512 devices in a mesh: tile: 64 (over z, x, y_lo), layer: 8 (over y_hi, core).
Axes of the slice: x: 4, y: 8 (y_hi: 4, y_lo: 2; y = y_hi * 2 + y_lo), z: 8, core: 2. Of those that a mesh axis runs over, the one named last changes fastest.
Arguments:
- screens: float32 [32, 1024, 2048], P('layer', 'tile'), may hold values from -4 to 4
- wind_shift: int32 [32, 2], replicated, may hold values from -16 to 383, as said below
- cone_offset: int32 [6, 32], replicated, may hold values from 0 to 383
- cone_weight: float32 [6, 32], replicated, may hold values from 0.5 to 1.5
- valid_mask: int32 [64, 80], P('tile', 'layer'), may hold values from 0 to 1
- reconstructor: bfloat16 [80, 64, 6, 2, 16384], P('layer', None, None, None, 'tile'), may hold values from -0.0234375 to 0.0234375
Outputs:
- slopes: float32 [64, 6, 2, 80], P('tile', None, None, 'layer')
- commands: float32 [16384], P('tile')
The draws below stay inside these ranges and needn't reach their ends.
Inputs may be any that keep to these rules, and one draw needn't show every extreme that they name: `wind_shift`: column 0 is a row shift; some layer shifts by 16 and some by -16. Column 1 is a column shift of 0 to 383, and some layer shifts by 384 - 1.
All inputs are finite; a program needn't handle non-finite values.
Results may differ from the reference program's by a relative error of at most 0.0029.
Values may be sent and summed in bfloat16 or wider, within the bound.
A program may use at most 128 MiB of HBM per device.

```python
import math
import jax
import jax.numpy as jnp
from jax import lax

STARS = 6
NP = 16
NF = 32
SUBCOLS = 80
WIDE = 2048
HALO = 16
LAYERS = 32
SUBROWS = 64
ROWS = 1024
MARGIN = 384
COMMANDS = 16384


def draw_wind_shift(key, part):
    key_rows, key_order, key_cols = jax.random.split(key, 3)
    row_shift = jax.random.randint(key_rows, (LAYERS,), -HALO, HALO + 1)
    ordering = jax.random.permutation(key_order, LAYERS)
    places = jnp.arange(LAYERS)
    row_shift = jnp.where(places == ordering[0], HALO, row_shift)
    row_shift = jnp.where(places == ordering[1], -HALO, row_shift)
    col_shift = jax.random.randint(key_cols, (LAYERS,), 0, MARGIN)
    col_shift = jnp.where(places == ordering[0], MARGIN - 1, col_shift)
    return jnp.stack([row_shift, col_shift], axis=1).astype(jnp.int32)


def draw_valid_mask(key, part):
    key_center, key_inner = jax.random.split(key, 2)
    centre_move = jax.random.randint(key_center, (), -2, 3)
    inner_level = jax.random.randint(key_inner, (), 1, 3)
    row_place = 2 * jnp.arange(SUBROWS)[:, None] + 1 - SUBROWS
    col_place = 2 * jnp.arange(SUBCOLS)[None, :] + 1 - SUBCOLS - 2 * centre_move
    distance = row_place * row_place * (SUBCOLS * SUBCOLS) + col_place * col_place * (SUBROWS * SUBROWS)
    whole = SUBROWS * SUBCOLS * (SUBROWS * SUBCOLS)
    inside = (20 * distance <= 21 * whole) & (16 * distance >= inner_level * whole)
    return inside.astype(jnp.int32)


def place_ends(entries, rng, low, high):
    longest = entries.shape.index(max(entries.shape))
    spots = []
    for shift in (0, 1):
        where = [jax.random.randint(jax.random.fold_in(rng, axis), (), 0, length) for axis, length in enumerate(entries.shape)]
        where[longest] = (where[longest] + shift) % entries.shape[longest]
        spots.append(tuple(where))
    return entries.at[spots[0]].set(low).at[spots[1]].set(high)


def levels(rng, extent, pieces, least, top_value):
    def one(axis_at, parts):
        draws = jax.random.uniform(jax.random.fold_in(jax.random.fold_in(rng, 6), axis_at), (parts,), jnp.float32, least / len(pieces), top_value / len(pieces))
        return jnp.repeat(jnp.exp(draws), extent[axis_at] // parts).reshape((-1,) + (1,) * (len(extent) - axis_at - 1))

    level = one(*pieces[0])
    for cut in pieces[1:]:
        level = level * one(*cut)
    return level


def gaussian(stream_key, extent, spread, reach, pieces=(), kind=jnp.bfloat16):
    level = levels(stream_key, extent, pieces, -0.22, 0.18) if pieces else 1.0
    array = jax.random.normal(stream_key, extent, jnp.float32) * spread * level
    return jnp.minimum(jnp.maximum(array, -reach), reach).astype(kind)


def setup_inputs(seed: int = 0) -> dict:
    key_of = jax.random.split(jax.random.key(seed), 7)
    return {
        "screens": gaussian(key_of[0], (LAYERS, ROWS, WIDE), 0.27, 4.0, ((0, 8), (1, 64)), jnp.float32),
        "wind_shift": draw_wind_shift(jax.random.fold_in(key_of[6], 71), 0),
        "cone_offset": place_ends(jax.random.randint(key_of[2], (STARS, LAYERS), 0, MARGIN), jax.random.fold_in(key_of[2], 1), 0, MARGIN - 1).astype(jnp.int32),
        "cone_weight": jnp.clip(jax.random.uniform(key_of[3], (STARS, LAYERS), jnp.float32, 0.5, 1.5), 0.5, 1.5),
        "valid_mask": draw_valid_mask(jax.random.fold_in(key_of[6], 71), 0),
        "reconstructor": gaussian(key_of[5], (SUBCOLS, SUBROWS, STARS, 2, COMMANDS), (2 * STARS * SUBROWS * SUBCOLS) ** -0.5, 0.0234375, ((0, 8), (4, 64))),
    }


def spot_tables(length, pixels):
    frequency = jnp.arange(length, dtype=jnp.float32) - length // 2
    sample = jnp.arange(pixels, dtype=jnp.float32)
    phase_angle = 2.0 * math.pi * frequency[:, None] * sample[None, :] / length
    return jnp.cos(phase_angle), -jnp.sin(phase_angle)


def centroids(phase_block):
    table_real, table_imag = spot_tables(NF, NP)
    highest = lax.Precision.HIGHEST
    field_real = jnp.cos(phase_block)
    field_imag = jnp.sin(phase_block)

    def left_side(table, field):
        return jnp.einsum('up,grpcq->grucq', table, field, precision=highest)

    def right_side(table, field):
        return jnp.einsum('vq,grucq->grucv', table, field, precision=highest)

    section_real = left_side(table_real, field_real) - left_side(table_imag, field_imag)
    section_imag = left_side(table_real, field_imag) + left_side(table_imag, field_real)
    spot_real = right_side(table_real, section_real) - right_side(table_imag, section_imag)
    spot_imag = right_side(table_imag, section_real) + right_side(table_real, section_imag)
    intensity = spot_real * spot_real + spot_imag * spot_imag
    centred = jnp.arange(NF, dtype=jnp.float32) - NF // 2
    totals = jnp.sum(intensity, axis=(2, 4))
    along_cols = jnp.einsum('grucv,v->grc', intensity, centred, precision=highest) / totals
    along_rows = jnp.einsum('grucv,u->grc', intensity, centred, precision=highest) / totals
    return jnp.stack([along_cols, along_rows], axis=2)


def reference(screens, wind_shift, cone_offset, cone_weight, valid_mask, reconstructor):
    pixel_rows = screens.shape[1]
    pupil_width = SUBCOLS * NP
    pupil_phase = jnp.zeros((STARS, pixel_rows, pupil_width), jnp.float32)
    for layer_index in range(LAYERS):
        moved = jnp.roll(screens[layer_index], wind_shift[layer_index, 0], axis=0)

        def per_star(amount):
            beginning = (wind_shift[layer_index, 1] + amount).astype(jnp.int32)
            return lax.dynamic_slice_in_dim(moved, beginning, pupil_width, 1)

        footprints = jax.vmap(per_star)(cone_offset[:, layer_index])
        pupil_phase = pupil_phase + cone_weight[:, layer_index][:, None, None] * footprints
    blocks = pupil_phase.reshape(STARS, SUBROWS, NP, SUBCOLS, NP)

    def one_star(star_block):
        return centroids(star_block[None])[0]

    star_slopes = lax.map(one_star, blocks)
    slopes = jnp.transpose(star_slopes, (1, 0, 2, 3))
    slopes = slopes * valid_mask[:, None, None, :].astype(jnp.float32)
    coarse = slopes.astype(jnp.bfloat16)

    def accumulate(running, column):
        block = reconstructor[column]
        vector = coarse[:, :, :, column].reshape(1, -1)
        product = jnp.dot(vector, block.reshape(vector.shape[1], -1), preferred_element_type=jnp.float32)
        return running + product[0], None

    commands, _ = lax.scan(accumulate, jnp.zeros((reconstructor.shape[4],), jnp.float32), jnp.arange(SUBCOLS))
    return slopes, commands
```

```python
import math

import jax
import jax.numpy as jnp
from jax import lax
from jax.experimental import pallas as pl
from jax.experimental.pallas import tpu as pltpu
from jax.sharding import PartitionSpec as P

STARS = 6
NP = 16
SPAN = 160
TILES = 64
UNIT = 2.0 * math.pi / 65536.0
MESH = pl.DeviceIdType.MESH
HIGHEST = lax.Precision.HIGHEST


def modulo_16(q):
    return ((q + 32768) & 65535) - 32768


def filter_tables():
    row = lax.broadcasted_iota(jnp.int32, (128, 128), 0)
    col = lax.broadcasted_iota(jnp.int32, (128, 128), 1)
    gap = row - col
    same = (row >> 4) == (col >> 4)
    sign = jnp.where((gap & 1) == 0, 1.0, -1.0)
    angle = gap.astype(jnp.float32) * (math.pi / 32.0)
    inside = jnp.where(same & (gap != 0), angle, math.pi / 2.0)
    cotangent = jnp.cos(inside) / jnp.sin(inside)
    flips = jnp.where(same, sign, 0.0)
    odd = jnp.where(same & (gap != 0), -16.0 * sign * cotangent, 0.0)
    return flips, odd


def dot(a, b):
    return jnp.dot(a, b, precision=HIGHEST, preferred_element_type=jnp.float32)


def footprint_kernel(wind, cone_offset, cone_weight, screens, coded_ref, rows_3, total):
    layer = lax.axis_index("layer")
    zeros = jnp.zeros((8, 128), jnp.float32)
    for slot in range(4):
        down = (wind[layer * 4 + slot, 0] + 16) % 8
        for m in range(16):
            columns = slice(128 * m, 128 * m + 128)
            band = jnp.concatenate([screens[slot, :, columns], zeros], axis=0)
            rows_3[slot, :, columns] = pltpu.roll(band, down, axis=0)

    lane = lax.broadcasted_iota(jnp.int32, (48, 128), 1)
    lane_24 = lax.broadcasted_iota(jnp.int32, (24, 128), 1)
    tails = [None] * 8
    for star in range(STARS):
        total[star] = jnp.zeros((56, 1280), jnp.float32)
        for slot in range(4):
            which = layer * 4 + slot
            beginning = wind[which, 1] + cone_offset[star, which]
            weight = cone_weight[star, which]
            base = beginning // 128
            turn = beginning % 128
            roll_by = (128 - turn) % 128
            stay = lane_24 < 128 - turn
            group = (wind[which, 0] + 16) // 8
            rows = pl.ds(pl.multiple_of(group * 8, 8), 24)

            def turned(m, slot=slot, base=base, roll_by=roll_by):
                columns = pl.ds(pl.multiple_of((base + m) * 128, 128), 128)
                return pltpu.roll(rows_3[slot, :, columns], roll_by, axis=1)

            before = turned(0)
            for m in range(10):
                after = turned(m + 1)
                columns = slice(128 * m, 128 * m + 128)
                total[star, rows, columns] = total[star, rows, columns] + weight * jnp.where(
                    stay, before, after
                )
                before = after
        code = [
            modulo_16(
                jnp.round(total[star, 0:48, 128 * m : 128 * m + 128] * (1.0 / UNIT)).astype(
                    jnp.int32
                )
            )
            for m in range(10)
        ]
        for block in range(8):
            first, start = (block * SPAN) // 128, (block * SPAN) % 128
            if start == 0:
                main = code[first]
            else:
                main = jnp.where(
                    lane < 128 - start,
                    pltpu.roll(code[first], 128 - start, axis=1),
                    pltpu.roll(code[first + 1], 128 - start, axis=1),
                )
            place = 32 * (star % 4)
            tail = code[first + 1]
            if place != start:
                tail = pltpu.roll(tail, (place - start) % 128, axis=1)
            tail = jnp.where((lane >= place) & (lane < place + 32), tail, 0)
            tails[block] = tail if star % 4 == 0 else tails[block] + tail
            for band in range(3):
                rows = slice(16 * band, 16 * band + 16)
                coded_ref[band, block, pl.ds(16 * star, 16), :] = main[rows].astype(jnp.int16)
                if star in (3, 5):
                    coded_ref[band, block, pl.ds(96 + 16 * (star // 4), 16), :] = tails[block][
                        rows
                    ].astype(jnp.int16)


def footprints(wind_shift, cone_offset, cone_weight, screens):
    return pl.pallas_call(
        footprint_kernel,
        out_shape=jax.ShapeDtypeStruct((3, 8, 128, 128), jnp.int16),
        in_specs=[
            pl.BlockSpec(memory_space=pltpu.SMEM),
            pl.BlockSpec(memory_space=pltpu.SMEM),
            pl.BlockSpec(memory_space=pltpu.SMEM),
            pl.BlockSpec(memory_space=pltpu.VMEM),
        ],
        out_specs=pl.BlockSpec(memory_space=pltpu.VMEM),
        scratch_shapes=[
            pltpu.VMEM((4, 24, 2048), jnp.float32),
            pltpu.VMEM((STARS, 56, 1280), jnp.float32),
        ],
        compiler_params=pltpu.CompilerParams(vmem_limit_bytes=16 * 1024 * 1024),
        name="footprints",
    )(wind_shift, cone_offset, cone_weight, screens)


def front_kernel(
    partial,
    mask_ref,
    slopes_ref,
    all_ref,
    swapped,
    coded,
    landed,
    plane,
    line,
    swap_send,
    swap_recv,
    code_send,
    code_recv,
    plane_send,
    plane_recv,
    line_send,
    line_recv,
):
    tile = lax.axis_index("tile")
    layer = lax.axis_index("layer")
    chip_y = layer // 2
    core = layer % 2
    half = layer // 4
    in_plane = tile % 8
    along = tile // 8

    def at(tile_index, layer_index):
        return (tile_index, layer_index)

    partner = at(tile, layer + 1 - 2 * core)

    def code_target(band, d):
        return at((tile + band - 1 + TILES) % TILES, core * 4 + d)

    def code_source(band, y):
        return at((tile - (band - 1) + TILES) % TILES, y * 2 + half)

    barrier = pltpu.get_barrier_semaphore()

    def greet(where):
        pl.semaphore_signal(barrier, inc=1, device_id=where, device_id_type=MESH)

    greet(partner)
    own_is_target = half == core
    for band in range(3):
        for y in range(4):
            if band == 1:
                @pl.when(jnp.logical_not(own_is_target & (chip_y == y)))
                def _(band=band, y=y):
                    greet(code_source(band, y))
            else:
                greet(code_source(band, y))
    for step in range(1, 8):
        greet(at(along * 8 + (in_plane + step) % 8, layer))
        greet(at(((along + step) % 8) * 8 + in_plane, layer))

    flips, odd = filter_tables()

    pl.semaphore_wait(barrier, 27 - own_is_target.astype(jnp.int32))

    def swap(band):
        return pltpu.make_async_remote_copy(
            src_ref=partial.at[band, pl.ds((1 - core) * 4, 4)],
            dst_ref=swapped.at[band],
            send_sem=swap_send.at[band],
            recv_sem=swap_recv.at[band],
            device_id=partner,
            device_id_type=MESH,
        )

    for band in range(3):
        swap(band).start()

    def code_copy(band, d):
        return pltpu.make_async_remote_copy(
            src_ref=coded.at[band, d],
            dst_ref=landed.at[band, chip_y],
            send_sem=code_send.at[band, d],
            recv_sem=code_recv.at[band, chip_y],
            device_id=code_target(band, d),
            device_id_type=MESH,
        )

    def arrival(band, y):
        return pltpu.make_async_remote_copy(
            src_ref=coded.at[band, 0],
            dst_ref=landed.at[band, y],
            send_sem=code_send.at[band, 0],
            recv_sem=code_recv.at[band, y],
            device_id=code_source(band, y),
            device_id_type=MESH,
        )

    for band in range(3):
        swap(band).wait_recv()
        for d in range(4):
            own = partial[band, core * 4 + d].astype(jnp.int32)
            both = own + swapped[band, d].astype(jnp.int32)
            coded[band, d] = modulo_16(both).astype(jnp.int16)
        for d in range(4):
            if band == 1:
                is_self = core * 4 + d == layer

                @pl.when(jnp.logical_not(is_self))
                def _(band=band, d=d):
                    code_copy(band, d).start()

                @pl.when(is_self)
                def _(band=band, d=d):
                    landed[band, chip_y] = coded[band, d]
            else:
                code_copy(band, d).start()

    for band in range(3):
        for y in range(4):
            if band == 1:
                @pl.when(jnp.logical_not(own_is_target & (chip_y == y)))
                def _(band=band, y=y):
                    arrival(band, y).wait_recv()
            else:
                arrival(band, y).wait_recv()

    phase_code = jnp.zeros((128, 128), jnp.int32)
    for band in range(3):
        for y in range(4):
            phase_code = phase_code + landed[band, y].astype(jnp.int32)
    phase = modulo_16(phase_code).astype(jnp.float32) * UNIT
    field_real = jnp.cos(phase)
    field_imag = jnp.sin(phase)
    along_cols = -16.0 * (
        field_real * dot(field_real, flips) + field_imag * dot(field_imag, flips)
    ) - 2.0 * field_imag * dot(field_real, odd)
    along_rows = -16.0 * (
        field_real * dot(flips, field_real) + field_imag * dot(flips, field_imag)
    ) + 2.0 * field_imag * dot(odd, field_real)

    lane_8 = lax.broadcasted_iota(jnp.int32, (8, 128), 1)
    row_8 = lax.broadcasted_iota(jnp.int32, (8, 128), 0)
    parts = []
    for moment in (along_cols, along_rows):
        blocks = jnp.sum(moment.reshape(8, 16, 128), axis=1)
        shared = jnp.where(row_8 < 4, blocks[6:7, :], blocks[7:8, :])
        shared = jnp.where((lane_8 >> 5) == (row_8 & 3), shared, 0.0)
        parts.append(jnp.concatenate([blocks, shared], axis=1))
    sums = jnp.concatenate(parts, axis=0)
    source = lax.broadcasted_iota(jnp.int32, (256, 128), 0)
    column = lax.broadcasted_iota(jnp.int32, (256, 128), 1) % 10
    wanted = jnp.where(
        source < 128, source >> 4, 8 + ((source >> 4) & 1)
    )
    pick = jnp.where(wanted == column, 1.0 / 8192.0, 0.0)
    pick = jnp.where((source >= 128) & (column < 8), 0.0, pick)
    spread = jnp.where(
        lax.broadcasted_iota(jnp.int32, (10, 128), 0)
        == lax.broadcasted_iota(jnp.int32, (10, 128), 1) % 10,
        1.0,
        0.0,
    )
    lit = dot(mask_ref[...].astype(jnp.float32), spread)
    measured = dot(sums, pick) * lit
    for star in range(STARS):
        for axis in range(2):
            slopes_ref[0, star, axis, :] = measured[axis * 8 + star, 0:10]
    lane_16 = lax.broadcasted_iota(jnp.int32, (16, 128), 1)
    row_16 = lax.broadcasted_iota(jnp.int32, (16, 128), 0)
    entry = (row_16 & 7) * 2 + (row_16 >> 3)
    coarse = measured.astype(jnp.bfloat16).astype(jnp.float32)
    flat = jnp.sum(jnp.where(lane_16 // 10 == entry, coarse, 0.0), axis=0, keepdims=True)
    plane[in_plane] = flat

    def plane_copy(step):
        other = (in_plane + step) % 8
        return pltpu.make_async_remote_copy(
            src_ref=plane.at[in_plane],
            dst_ref=plane.at[in_plane],
            send_sem=plane_send.at[step],
            recv_sem=plane_recv.at[step],
            device_id=at(along * 8 + other, layer),
            device_id_type=MESH,
        )

    def plane_arrival(step):
        other = (in_plane - step + 8) % 8
        return pltpu.make_async_remote_copy(
            src_ref=plane.at[in_plane],
            dst_ref=plane.at[other],
            send_sem=plane_send.at[step],
            recv_sem=plane_recv.at[step],
            device_id=at(along * 8 + other, layer),
            device_id_type=MESH,
        )

    for step in range(1, 8):
        plane_copy(step).start()
    for step in range(1, 8):
        plane_arrival(step).wait_recv()

    def line_copy(step):
        return pltpu.make_async_remote_copy(
            src_ref=plane,
            dst_ref=line.at[along],
            send_sem=line_send.at[step],
            recv_sem=line_recv.at[step],
            device_id=at(((along + step) % 8) * 8 + in_plane, layer),
            device_id_type=MESH,
        )

    def line_arrival(step):
        other = (along - step + 8) % 8
        return pltpu.make_async_remote_copy(
            src_ref=plane,
            dst_ref=line.at[other],
            send_sem=line_send.at[step],
            recv_sem=line_recv.at[step],
            device_id=at(other * 8 + in_plane, layer),
            device_id_type=MESH,
        )

    for step in range(1, 8):
        line_copy(step).start()
    line[along] = plane[...]
    for step in range(1, 8):
        line_arrival(step).wait_recv()
    all_ref[...] = line[...].reshape(TILES, 1, 128)

    for band in range(3):
        swap(band).wait_send()
        for d in range(4):
            if band == 1:
                @pl.when(jnp.logical_not(core * 4 + d == layer))
                def _(band=band, d=d):
                    code_copy(band, d).wait_send()
            else:
                code_copy(band, d).wait_send()
    for step in range(1, 8):
        plane_copy(step).wait_send()
        line_copy(step).wait_send()


def front(partial, valid_mask):
    dma = pltpu.SemaphoreType.DMA
    return pl.pallas_call(
        front_kernel,
        out_shape=(
            jax.ShapeDtypeStruct((1, STARS, 2, 10), jnp.float32),
            jax.ShapeDtypeStruct((TILES, 1, 128), jnp.float32),
        ),
        in_specs=[pl.BlockSpec(memory_space=pltpu.VMEM)] * 2,
        out_specs=(
            pl.BlockSpec(memory_space=pltpu.VMEM),
            pl.BlockSpec(memory_space=pltpu.VMEM),
        ),
        scratch_shapes=[
            pltpu.VMEM((3, 4, 128, 128), jnp.int16),
            pltpu.VMEM((3, 4, 128, 128), jnp.int16),
            pltpu.VMEM((3, 4, 128, 128), jnp.int16),
            pltpu.VMEM((8, 1, 128), jnp.float32),
            pltpu.VMEM((8, 8, 1, 128), jnp.float32),
            dma((3,)),
            dma((3,)),
            dma((3, 4)),
            dma((3, 4)),
            dma((8,)),
            dma((8,)),
            dma((8,)),
            dma((8,)),
        ],
        compiler_params=pltpu.CompilerParams(
            collective_id=0, has_side_effects=True, vmem_limit_bytes=16 * 1024 * 1024
        ),
        name="front",
    )(partial, valid_mask)


def sum_kernel(part_ref, out_ref, rows, send_sem, recv_sem):
    tile = lax.axis_index("tile")
    layer = lax.axis_index("layer")
    barrier = pltpu.get_barrier_semaphore()
    for step in range(1, 8):
        pl.semaphore_signal(
            barrier, inc=1, device_id=(tile, (layer + step) % 8), device_id_type=MESH
        )
    pl.semaphore_wait(barrier, 7)

    def copy(step):
        return pltpu.make_async_remote_copy(
            src_ref=part_ref,
            dst_ref=rows.at[layer],
            send_sem=send_sem.at[step],
            recv_sem=recv_sem.at[step],
            device_id=(tile, (layer + step) % 8),
            device_id_type=MESH,
        )

    def arrival(step):
        other = (layer - step + 8) % 8
        return pltpu.make_async_remote_copy(
            src_ref=part_ref,
            dst_ref=rows.at[other],
            send_sem=send_sem.at[step],
            recv_sem=recv_sem.at[step],
            device_id=(tile, other),
            device_id_type=MESH,
        )

    for step in range(1, 8):
        copy(step).start()
    rows[layer] = part_ref[...]
    for step in range(1, 8):
        arrival(step).wait_recv()
    total = rows[0]
    for k in range(1, 8):
        total = total + rows[k]
    out_ref[...] = total
    for step in range(1, 8):
        copy(step).wait_send()


def sum_over_layers(partial):
    dma = pltpu.SemaphoreType.DMA
    return pl.pallas_call(
        sum_kernel,
        out_shape=jax.ShapeDtypeStruct(partial.shape, jnp.float32),
        in_specs=[pl.BlockSpec(memory_space=pltpu.VMEM)],
        out_specs=pl.BlockSpec(memory_space=pltpu.VMEM),
        scratch_shapes=[
            pltpu.VMEM((8,) + partial.shape, jnp.float32),
            dma((8,)),
            dma((8,)),
        ],
        compiler_params=pltpu.CompilerParams(collective_id=1, has_side_effects=True),
        name="sum_over_layers",
    )(partial)


def on_device(screens, wind_shift, cone_offset, cone_weight, valid_mask, reconstructor):
    partial = footprints(wind_shift, cone_offset, cone_weight, screens)
    slopes, gathered = front(partial, valid_mask)
    coarse = gathered[:, 0, :120].astype(jnp.bfloat16).reshape(TILES, STARS, 2, 10)
    partial = jnp.einsum(
        "jrgac,rgaj->c", reconstructor, coarse, preferred_element_type=jnp.float32
    )
    commands = sum_over_layers(partial.reshape(1, -1)).reshape(-1)
    return slopes, commands


def solution(mesh):
    placed = (
        P("layer", "tile", None),
        P(),
        P(),
        P(),
        P("tile", "layer"),
        P("layer", None, None, None, "tile"),
    )
    return jax.shard_map(
        on_device,
        mesh=mesh,
        in_specs=placed,
        out_specs=(P("tile", None, None, "layer"), P("tile")),
        check_vma=False,
    )
```

```python
import math

import jax
import jax.numpy as jnp
from jax import lax
from jax.experimental import pallas as pl
from jax.experimental.pallas import tpu as pltpu
from jax.sharding import PartitionSpec as P

STARS = 6
SPAN = 160
TILES = 64
UNIT = 2.0 * math.pi / 65536.0
MESH = pl.DeviceIdType.MESH
F32 = jnp.float32
BF16 = jnp.bfloat16
SINE = (
    1.5707962900208665,
    -0.6459633598429161,
    0.07968848044711395,
    -0.0046722277849454265,
    0.00015082049685476598,
)


def modulo_16(q):
    return ((q + 32768) & 65535) - 32768


def iota(shape, axis):
    return lax.broadcasted_iota(jnp.int32, shape, axis)


def split(x):
    high = x.astype(BF16)
    return high, (x - high.astype(F32)).astype(BF16)


def dot(a, b):
    return jnp.dot(a, b, preferred_element_type=F32)


def sine(q):
    q = jnp.where(q > 16384, 32768 - q, jnp.where(q < -16384, -32768 - q, q))
    x = q.astype(F32) * (1.0 / 16384.0)
    square = x * x
    value = SINE[4]
    for coefficient in SINE[3::-1]:
        value = value * square + coefficient
    return value * x


def filter_tables():
    row = iota((128, 128), 0)
    col = iota((128, 128), 1)
    gap = row - col
    same = (row >> 4) == (col >> 4)
    sign = jnp.where((gap & 1) == 0, 1.0, -1.0)
    angle = gap.astype(F32) * (math.pi / 32.0)
    inside = jnp.where(same & (gap != 0), angle, math.pi / 2.0)
    cotangent = jnp.cos(inside) / jnp.sin(inside)
    flips = jnp.where(same, sign, 0.0)
    odd = jnp.where(same & (gap != 0), -16.0 * sign * cotangent, 0.0)
    return flips, odd


def frame_kernel(
    whole_ref,
    cone_weight,
    lit_ref_in,
    screens_hbm,
    matrix_hbm,
    slopes_ref,
    commands_ref,
    held,
    placed,
    partial,
    swapped,
    coded,
    landed,
    filters,
    low_filter,
    pick_ref,
    lit_ref,
    expand,
    keep,
    plane,
    line,
    matrix,
    own_part,
    parts,
    load_sem,
    swap_send,
    swap_recv,
    code_send,
    code_recv,
    plane_send,
    plane_recv,
    line_send,
    line_recv,
    part_send,
    part_recv,
):
    tile = lax.axis_index("tile")
    layer = lax.axis_index("layer")
    chip_y = layer // 2
    core = layer % 2
    half = layer // 4
    in_plane = tile % 8
    along = tile // 8

    def at(tile_index, layer_index):
        return (tile_index, layer_index)

    partner = at(tile, layer + 1 - 2 * core)

    def code_target(band, d):
        return at((tile + band - 1 + TILES) % TILES, core * 4 + d)

    def code_source(band, y):
        return at((tile - (band - 1) + TILES) % TILES, y * 2 + half)

    def plane_peer(step):
        return at(along * 8 + (in_plane + step + 8) % 8, layer)

    def line_peer(step):
        return at(((along + step + 8) % 8) * 8 + in_plane, layer)

    def layer_peer(step):
        return at(tile, (layer + step + 8) % 8)

    barrier = pltpu.get_barrier_semaphore()

    def greet(where):
        pl.semaphore_signal(barrier, inc=1, device_id=where, device_id_type=MESH)

    greet(partner)
    own_is_target = half == core
    for band in range(3):
        for y in range(4):
            if band == 1:
                @pl.when(jnp.logical_not(own_is_target & (chip_y == y)))
                def _(band=band, y=y):
                    greet(code_source(band, y))
            else:
                greet(code_source(band, y))
    for step in range(1, 8):
        greet(plane_peer(-step))
        greet(line_peer(-step))
        greet(layer_peer(-step))

    screens_load = pltpu.make_async_copy(screens_hbm, held, load_sem.at[0])
    screens_load.start()
    matrix_load = pltpu.make_async_copy(matrix_hbm, matrix, load_sem.at[1])
    matrix_load.start()

    zeros = jnp.zeros((32, 128), F32)
    screens_load.wait()
    for slot in range(4):
        down = whole_ref[0, layer * 4 + slot] + 16
        for m in range(16):
            rows = held[16 * slot : 16 * slot + 16, 128 * m : 128 * m + 128]
            placed[16 * slot + m] = pltpu.roll(
                jnp.concatenate([rows, zeros], axis=0), down, axis=0
            )

    lane = iota((48, 128), 1)

    def add_layers(which_half):
        tails = [None] * 4
        for star in range(STARS):
            total = [None] * 5
            for slot in range(4):
                which = layer * 4 + slot
                beginning = whole_ref[1, which] + whole_ref[2 + star, which]
                weight = cone_weight[star, which]
                first = lax.shift_right_logical(beginning, 7) + 5 * which_half + 16 * slot
                turn = beginning & 127
                roll_by = (128 - turn) & 127
                stay = lane < 128 - turn
                before = pltpu.roll(placed[first], roll_by, axis=1)
                for m in range(5):
                    after = pltpu.roll(placed[first + m + 1], roll_by, axis=1)
                    term = weight * jnp.where(stay, before, after)
                    total[m] = term if slot == 0 else total[m] + term
                    before = after
            code = [
                modulo_16(jnp.round(part * (1.0 / UNIT)).astype(jnp.int32)) for part in total
            ]
            for d in range(4):
                start = 32 * d
                main = code[d]
                if d > 0:
                    main = jnp.where(
                        lane < 128 - start,
                        pltpu.roll(code[d], 128 - start, axis=1),
                        pltpu.roll(code[d + 1], 128 - start, axis=1),
                    )
                place = 32 * (star % 4)
                tail = code[d + 1]
                if place != start:
                    tail = pltpu.roll(tail, (place - start) % 128, axis=1)
                tail = jnp.where((lane >= place) & (lane < place + 32), tail, 0)
                tails[d] = tail if star % 4 == 0 else tails[d] + tail
                for band in range(3):
                    rows = slice(16 * band, 16 * band + 16)
                    block = 4 * which_half + d
                    partial[band, block, 16 * star : 16 * star + 16, :] = main[rows].astype(
                        jnp.int16
                    )
                    if star in (3, 5):
                        at_row = 96 + 16 * (star // 4)
                        partial[band, block, at_row : at_row + 16, :] = tails[d][rows].astype(
                            jnp.int16
                        )

    def remote(source, target, send, recv, where):
        return pltpu.make_async_remote_copy(
            src_ref=source,
            dst_ref=target,
            send_sem=send,
            recv_sem=recv,
            device_id=where,
            device_id_type=MESH,
        )

    def swap(band):
        return remote(
            partial.at[band, pl.ds((1 - core) * 4, 4)],
            swapped.at[band],
            swap_send.at[band],
            swap_recv.at[band],
            partner,
        )

    def code_copy(band, d):
        return remote(
            coded.at[band, d],
            landed.at[band, chip_y],
            code_send.at[band, d],
            code_recv.at[band, chip_y],
            code_target(band, d),
        )

    def code_arrival(band, y):
        return remote(
            coded.at[band, 0],
            landed.at[band, y],
            code_send.at[band, 0],
            code_recv.at[band, y],
            code_source(band, y),
        )

    add_layers(1 - core)
    pl.semaphore_wait(barrier, 34 - own_is_target.astype(jnp.int32))
    for band in range(3):
        swap(band).start()
    add_layers(core)

    for band in range(3):
        swap(band).wait_recv()
        for d in range(4):
            own = partial[band, core * 4 + d].astype(jnp.int32)
            both = own + swapped[band, d].astype(jnp.int32)
            coded[band, d] = modulo_16(both).astype(jnp.int16)
        for d in range(4):
            if band == 1:
                is_self = core * 4 + d == layer

                @pl.when(jnp.logical_not(is_self))
                def _(band=band, d=d):
                    code_copy(band, d).start()

                @pl.when(is_self)
                def _(band=band, d=d):
                    landed[band, chip_y] = coded[band, d]
            else:
                code_copy(band, d).start()

    flips, odd = filter_tables()
    odd_high, odd_low = split(odd)
    filters[0] = flips.astype(BF16)
    filters[1] = odd_high
    low_filter[...] = odd_low
    column = iota((256, 384), 1)
    column = jnp.where(column < 128, column, (column - 128) >> 4)
    source = iota((256, 384), 0)
    wanted = jnp.where(source < 128, source >> 4, 8 + ((source >> 4) & 1))
    pick_ref[...] = jnp.where(wanted == column, 1.0 / 8192.0, 0.0).astype(BF16)
    spread = jnp.where(iota((10, 384), 0) == column[0:10], 1.0, 0.0)
    lit_ref[...] = dot(lit_ref_in[...].astype(F32), spread)
    place = iota((64, 1536), 1)
    begin = 24 * iota((64, 1536), 0)
    expand[...] = jnp.where((place >= begin) & (place < begin + 24), 1.0, 0.0).astype(BF16)
    place = iota((16, 1536), 1)
    entry = ((place >> 2) % 6) * 2 + (place & 1)
    for h in range(2):
        wanted = (entry == iota((16, 1536), 0)) & (((place >> 1) & 1) == h)
        keep[h] = jnp.where(wanted, 1.0, 0.0)

    for band in range(3):
        for y in range(4):
            if band == 1:
                @pl.when(jnp.logical_not(own_is_target & (chip_y == y)))
                def _(band=band, y=y):
                    code_arrival(band, y).wait_recv()
            else:
                code_arrival(band, y).wait_recv()

    code = jnp.zeros((128, 128), jnp.int32)
    for band in range(3):
        for y in range(4):
            code = code + landed[band, y].astype(jnp.int32)
    code = modulo_16(code)
    field_imag = sine(code)
    field_real = sine(modulo_16(code + 16384))
    real_high, real_low = split(field_real)
    imag_high, imag_low = split(field_imag)
    right = jnp.concatenate([filters[0], filters[1]], axis=1)
    across = dot(jnp.concatenate([real_high, real_low, imag_high, imag_low], axis=0), right)
    flipped_real = across[0:128, 0:128] + across[128:256, 0:128]
    flipped_imag = across[256:384, 0:128] + across[384:512, 0:128]
    turned_real = (
        across[0:128, 128:256] + across[128:256, 128:256] + dot(real_high, low_filter[...])
    )
    along_cols = (
        -16.0 * (field_real * flipped_real + field_imag * flipped_imag)
        - 2.0 * field_imag * turned_real
    )
    left = jnp.concatenate([filters[0], filters[1]], axis=0)
    down = dot(left, jnp.concatenate([real_high, real_low, imag_high, imag_low], axis=1))
    flipped_real = down[0:128, 0:128] + down[0:128, 128:256]
    flipped_imag = down[0:128, 256:384] + down[0:128, 384:512]
    turned_real = (
        down[128:256, 0:128] + down[128:256, 128:256] + dot(low_filter[...], real_high)
    )
    along_rows = (
        -16.0 * (field_real * flipped_real + field_imag * flipped_imag)
        + 2.0 * field_imag * turned_real
    )

    lane_8 = iota((8, 128), 1)
    row_8 = iota((8, 128), 0)
    sums = []
    for moment in (along_cols, along_rows):
        blocks = jnp.sum(moment.reshape(8, 16, 128), axis=1)
        shared = jnp.where(row_8 < 4, blocks[6:7, :], blocks[7:8, :])
        shared = jnp.where((lane_8 >> 5) == (row_8 & 3), shared, 0.0)
        sums.append(jnp.concatenate([blocks, shared], axis=1))
    sums = jnp.concatenate(sums, axis=0)
    high, rest = sums.astype(BF16), sums
    rest = rest - high.astype(F32)
    middle, low = split(rest)
    measured = dot(jnp.concatenate([high, middle, low], axis=0), pick_ref[...])
    measured = (measured[0:16] + measured[16:32] + measured[32:48]) * lit_ref[...]
    for star in range(STARS):
        for axis in range(2):
            slopes_ref[0, star, axis, :] = measured[axis * 8 + star, 0:10]
    lane_16 = iota((16, 256), 1)
    row_16 = iota((16, 256), 0)
    entry = (row_16 & 7) * 2 + (row_16 >> 3)
    coarse = measured[:, 128:384].astype(BF16).astype(F32)
    flat = jnp.where(((lane_16 & 15) == entry) & (entry < 12), coarse, 0.0)
    plane[in_plane] = jnp.sum(flat, axis=0, keepdims=True)

    def plane_copy(step):
        return remote(
            plane.at[in_plane],
            plane.at[in_plane],
            plane_send.at[step],
            plane_recv.at[step],
            plane_peer(step),
        )

    def plane_arrival(step):
        other = (in_plane - step + 8) % 8
        return remote(
            plane.at[in_plane],
            plane.at[other],
            plane_send.at[step],
            plane_recv.at[step],
            plane_peer(-step),
        )

    for step in range(1, 8):
        plane_copy(step).start()
    for step in range(1, 8):
        plane_arrival(step).wait_recv()

    def line_copy(step):
        return remote(
            plane, line.at[along], line_send.at[step], line_recv.at[step], line_peer(step)
        )

    def line_arrival(step):
        other = (along - step + 8) % 8
        return remote(
            plane, line.at[other], line_send.at[step], line_recv.at[step], line_peer(-step)
        )

    for step in range(1, 8):
        line_copy(step).start()
    line[along] = plane[...]
    for step in range(1, 8):
        line_arrival(step).wait_recv()

    matrix_load.wait()
    gathered = line[...].reshape(TILES, 256).astype(BF16)
    rows = lax.dot_general(
        gathered[:, 0:160],
        expand[...],
        (((0,), (0,)), ((), ())),
        preferred_element_type=F32,
    )
    total = jnp.zeros((32, 128), F32)
    for j in range(10):
        block = rows[16 * j : 16 * j + 16]
        vector = jnp.concatenate([block * keep[0], block * keep[1]], axis=0).astype(BF16)
        total = total + dot(vector, matrix[1536 * j : 1536 * j + 1536, :])
    own_part[...] = jnp.concatenate(
        [
            jnp.sum(total[0:16], axis=0, keepdims=True),
            jnp.sum(total[16:32], axis=0, keepdims=True),
        ],
        axis=1,
    )

    def part_copy(step):
        return remote(
            own_part, parts.at[layer], part_send.at[step], part_recv.at[step], layer_peer(step)
        )

    def part_arrival(step):
        other = (layer - step + 8) % 8
        return remote(
            own_part, parts.at[other], part_send.at[step], part_recv.at[step], layer_peer(-step)
        )

    for step in range(1, 8):
        part_copy(step).start()
    parts[layer] = own_part[...]
    for step in range(1, 8):
        part_arrival(step).wait_recv()
    total = parts[0]
    for k in range(1, 8):
        total = total + parts[k]
    commands_ref[...] = total

    for band in range(3):
        swap(band).wait_send()
        for d in range(4):
            if band == 1:
                @pl.when(jnp.logical_not(core * 4 + d == layer))
                def _(band=band, d=d):
                    code_copy(band, d).wait_send()
            else:
                code_copy(band, d).wait_send()
    for step in range(1, 8):
        plane_copy(step).wait_send()
        line_copy(step).wait_send()
        part_copy(step).wait_send()


def on_device(screens, wind_shift, cone_offset, cone_weight, valid_mask, reconstructor):
    dma = pltpu.SemaphoreType.DMA
    matrix = reconstructor.reshape(3840, 2, 2, 128).transpose(0, 2, 1, 3).reshape(15360, 128)
    slopes, commands = pl.pallas_call(
        frame_kernel,
        out_shape=(
            jax.ShapeDtypeStruct((1, STARS, 2, 10), F32),
            jax.ShapeDtypeStruct((1, 256), F32),
        ),
        in_specs=[
            pl.BlockSpec(memory_space=pltpu.SMEM),
            pl.BlockSpec(memory_space=pltpu.SMEM),
            pl.BlockSpec(memory_space=pltpu.VMEM),
            pl.BlockSpec(memory_space=pltpu.HBM),
            pl.BlockSpec(memory_space=pltpu.HBM),
        ],
        out_specs=[pl.BlockSpec(memory_space=pltpu.VMEM)] * 2,
        scratch_shapes=[
            pltpu.VMEM((64, 2048), F32),
            pltpu.VMEM((64, 48, 128), F32),
            pltpu.VMEM((3, 8, 128, 128), jnp.int16),
            pltpu.VMEM((3, 4, 128, 128), jnp.int16),
            pltpu.VMEM((3, 4, 128, 128), jnp.int16),
            pltpu.VMEM((3, 4, 128, 128), jnp.int16),
            pltpu.VMEM((2, 128, 128), BF16),
            pltpu.VMEM((128, 128), BF16),
            pltpu.VMEM((256, 384), BF16),
            pltpu.VMEM((1, 384), F32),
            pltpu.VMEM((64, 1536), BF16),
            pltpu.VMEM((2, 16, 1536), F32),
            pltpu.VMEM((8, 1, 256), F32),
            pltpu.VMEM((8, 8, 1, 256), F32),
            pltpu.VMEM((15360, 128), BF16),
            pltpu.VMEM((1, 256), F32),
            pltpu.VMEM((8, 1, 256), F32),
            dma((2,)),
            dma((3,)),
            dma((3,)),
            dma((3, 4)),
            dma((3, 4)),
            dma((8,)),
            dma((8,)),
            dma((8,)),
            dma((8,)),
            dma((8,)),
            dma((8,)),
        ],
        compiler_params=pltpu.CompilerParams(
            collective_id=0, has_side_effects=True, vmem_limit_bytes=66_900_000
        ),
        name="frame",
    )(
        jnp.concatenate([wind_shift.T, cone_offset], axis=0),
        cone_weight,
        valid_mask,
        screens.reshape(64, 2048),
        matrix,
    )
    return slopes, commands.reshape(-1)


def solution(mesh):
    placed = (
        P("layer", "tile", None),
        P(),
        P(),
        P(),
        P("tile", "layer"),
        P("layer", None, None, None, "tile"),
    )
    return jax.shard_map(
        on_device,
        mesh=mesh,
        in_specs=placed,
        out_specs=(P("tile", None, None, "layer"), P("tile")),
        check_vma=False,
    )
```

```python
import math

import jax
import jax.numpy as jnp
from jax import lax
from jax.experimental import pallas as pl
from jax.experimental.pallas import tpu as pltpu
from jax.sharding import PartitionSpec as P

STARS = 6
SPAN = 160
TILES = 64
UNIT = 2.0 * math.pi / 65536.0
MESH = pl.DeviceIdType.MESH
F32 = jnp.float32
BF16 = jnp.bfloat16
SINE = (
    1.5707962900208665,
    -0.6459633598429161,
    0.07968848044711395,
    -0.0046722277849454265,
    0.00015082049685476598,
)


def modulo_16(q):
    return ((q + 32768) & 65535) - 32768


def iota(shape, axis):
    return lax.broadcasted_iota(jnp.int32, shape, axis)


def split(x):
    high = x.astype(BF16)
    return high, (x - high.astype(F32)).astype(BF16)


def dot(a, b):
    return jnp.dot(a, b, preferred_element_type=F32)


def sine(q):
    q = jnp.where(q > 16384, 32768 - q, jnp.where(q < -16384, -32768 - q, q))
    x = q.astype(F32) * (1.0 / 16384.0)
    square = x * x
    value = SINE[4]
    for coefficient in SINE[3::-1]:
        value = value * square + coefficient
    return value * x


def filter_tables():
    row = iota((128, 128), 0)
    col = iota((128, 128), 1)
    gap = row - col
    same = (row >> 4) == (col >> 4)
    sign = jnp.where((gap & 1) == 0, 1.0, -1.0)
    angle = gap.astype(F32) * (math.pi / 32.0)
    inside = jnp.where(same & (gap != 0), angle, math.pi / 2.0)
    cotangent = jnp.cos(inside) / jnp.sin(inside)
    flips = jnp.where(same, sign, 0.0)
    odd = jnp.where(same & (gap != 0), -16.0 * sign * cotangent, 0.0)
    return flips, odd


def frame_kernel(
    wind_hbm,
    offset_hbm,
    weight_hbm,
    mask_hbm,
    screens_hbm,
    matrix_hbm,
    slopes_ref,
    commands_ref,
    wind,
    cone_offset,
    cone_weight,
    mask_ref,
    held,
    placed,
    partial,
    swapped,
    crossed,
    coded,
    landed,
    filters,
    low_filter,
    pick_ref,
    lit_ref,
    expand,
    keep,
    plane,
    line,
    matrix,
    own_part,
    parts,
    load_sem,
    swap_send,
    swap_recv,
    cross_send,
    cross_recv,
    code_send,
    code_recv,
    plane_send,
    plane_recv,
    line_send,
    line_recv,
    part_send,
    part_recv,
):
    tile = lax.axis_index("tile")
    layer = lax.axis_index("layer")
    chip_y = layer // 2
    core = layer % 2
    half = layer // 4
    in_plane = tile % 8
    along = tile // 8

    def at(tile_index, layer_index):
        return (tile_index, layer_index)

    partner = at(tile, layer + 1 - 2 * core)
    side = tile % 2
    near_tile = tile + 1 - 2 * side
    near_band = 2 - 2 * side
    far_band = 2 * side
    onward = at((tile + 4 * side - 2 + TILES) % TILES, layer)
    backward = at((tile - 4 * side + 2 + TILES) % TILES, layer)

    def code_target(near, d):
        return at(near_tile if near else tile, core * 4 + d)

    def code_source(near, y):
        return at(near_tile if near else tile, y * 2 + half)

    def plane_peer(step):
        return at(along * 8 + (in_plane + step + 8) % 8, layer)

    def line_peer(step):
        return at(((along + step + 8) % 8) * 8 + in_plane, layer)

    def layer_peer(step):
        return at(tile, (layer + step + 8) % 8)

    barrier = pltpu.get_barrier_semaphore()
    loads = [
        pltpu.make_async_copy(source, target, load_sem.at[k])
        for k, (source, target) in enumerate(
            (
                (screens_hbm, held),
                (wind_hbm, wind),
                (offset_hbm, cone_offset),
                (weight_hbm, cone_weight),
                (mask_hbm, mask_ref),
                (matrix_hbm, matrix),
            )
        )
    ]
    for load in loads:
        load.start()

    def greet(where):
        pl.semaphore_signal(barrier, inc=1, device_id=where, device_id_type=MESH)

    greet(partner)
    greet(backward)
    own_is_target = half == core
    for y in range(4):
        greet(code_source(True, y))

        @pl.when(jnp.logical_not(own_is_target & (chip_y == y)))
        def _(y=y):
            greet(code_source(False, y))

    for step in range(1, 8):
        greet(plane_peer(-step))
        greet(line_peer(-step))
        greet(layer_peer(-step))

    zeros = jnp.zeros((5, 8, 128), F32)

    def clear(k, carry):
        placed[pl.ds(11 * k, 5)] = zeros
        placed[pl.ds(11 * k + 8, 3)] = zeros[0:3]
        return carry

    lax.fori_loop(0, 64, clear, 0, unroll=8)
    for load in loads[:4]:
        load.wait()
    row = iota((8, 128), 0)
    for slot in range(4):
        down = (wind[0, layer * 4 + slot] + 16) & 7
        early = row < down
        for m in range(16):
            columns = slice(128 * m, 128 * m + 128)
            upper = pltpu.roll(held[16 * slot : 16 * slot + 8, columns], down, axis=0)
            lower = pltpu.roll(held[16 * slot + 8 : 16 * slot + 16, columns], down, axis=0)
            group = 11 * (16 * slot + m) + 5
            placed[group] = jnp.where(early, 0.0, upper)
            placed[group + 1] = jnp.where(early, upper, lower)
            placed[group + 2] = jnp.where(early, lower, 0.0)

    lane = iota((48, 128), 1)

    def add_layers(which_half):
        tails = [None] * 4
        for star in range(STARS):
            total = [None] * 5
            for slot in range(4):
                which = layer * 4 + slot
                beginning = wind[1, which] + cone_offset[star, which]
                weight = cone_weight[star, which]
                column = lax.shift_right_logical(beginning, 7) + 5 * which_half + 16 * slot
                first = 11 * column + 5 - lax.shift_right_logical(wind[0, which] + 16, 3)
                turn = beginning & 127
                roll_by = (128 - turn) & 127
                stay = lane < 128 - turn

                def turned(m, first=first, roll_by=roll_by):
                    window = placed[pl.ds(first + 11 * m, 6)].reshape(48, 128)
                    return pltpu.roll(window, roll_by, axis=1)

                before = turned(0)
                for m in range(5):
                    after = turned(m + 1)
                    term = weight * jnp.where(stay, before, after)
                    total[m] = term if slot == 0 else total[m] + term
                    before = after
            code = [jnp.round(part * (1.0 / UNIT)).astype(jnp.int32) for part in total]
            for d in range(4):
                start = 32 * d
                main = code[d]
                if d > 0:
                    main = jnp.where(
                        lane < 128 - start,
                        pltpu.roll(code[d], 128 - start, axis=1),
                        pltpu.roll(code[d + 1], 128 - start, axis=1),
                    )
                place = 32 * (star % 4)
                tail = code[d + 1]
                if place != start:
                    tail = pltpu.roll(tail, (place - start) % 128, axis=1)
                tail = jnp.where((lane >= place) & (lane < place + 32), tail, 0)
                tails[d] = tail if star % 4 == 0 else tails[d] + tail
                for band in range(3):
                    rows = slice(16 * band, 16 * band + 16)
                    block = 4 * which_half + d
                    partial[band, block, 16 * star : 16 * star + 16, :] = main[rows].astype(
                        jnp.int16
                    )
                    if star in (3, 5):
                        at_row = 96 + 16 * (star // 4)
                        partial[band, block, at_row : at_row + 16, :] = tails[d][rows].astype(
                            jnp.int16
                        )

    def remote(source, target, send, recv, where):
        return pltpu.make_async_remote_copy(
            src_ref=source,
            dst_ref=target,
            send_sem=send,
            recv_sem=recv,
            device_id=where,
            device_id_type=MESH,
        )

    def swap(band):
        return remote(
            partial.at[band, pl.ds((1 - core) * 4, 4)],
            swapped.at[band],
            swap_send.at[band],
            swap_recv.at[band],
            partner,
        )

    def cross(d):
        return remote(
            coded.at[far_band, d], crossed.at[d], cross_send.at[d], cross_recv.at[d], onward
        )

    def code_copy(near, d):
        return remote(
            coded.at[near_band if near else 1, d],
            landed.at[near, chip_y],
            code_send.at[near, d],
            code_recv.at[near, chip_y],
            code_target(near, d),
        )

    def code_arrival(near, y):
        return remote(
            coded.at[near_band if near else 1, 0],
            landed.at[near, y],
            code_send.at[near, 0],
            code_recv.at[near, y],
            code_source(near, y),
        )

    add_layers(1 - core)
    pl.semaphore_wait(barrier, 31 - own_is_target.astype(jnp.int32))
    for band in (far_band, 1, near_band):
        swap(band).start()
    add_layers(core)

    def both(band, d):
        own = partial[band, core * 4 + d].astype(jnp.int32)
        return own + swapped[band, d].astype(jnp.int32)

    swap(far_band).wait_recv()
    for d in range(4):
        coded[far_band, d] = both(far_band, d).astype(jnp.int16)
        cross(d).start()
    swap(1).wait_recv()
    for d in range(4):
        coded[1, d] = both(1, d).astype(jnp.int16)
    for d in range(4):
        is_self = core * 4 + d == layer

        @pl.when(jnp.logical_not(is_self))
        def _(d=d):
            code_copy(0, d).start()

        @pl.when(is_self)
        def _(d=d):
            landed[0, chip_y] = coded[1, d]

    swap(near_band).wait_recv()
    for d in range(4):
        cross(d).wait_recv()
        total = both(near_band, d) + crossed[d].astype(jnp.int32)
        coded[near_band, d] = total.astype(jnp.int16)
        code_copy(1, d).start()

    flips, odd = filter_tables()
    odd_high, odd_low = split(odd)
    filters[0] = flips.astype(BF16)
    filters[1] = odd_high
    low_filter[...] = odd_low
    column = iota((256, 384), 1)
    column = jnp.where(column < 128, column, (column - 128) >> 4)
    source = iota((256, 384), 0)
    wanted = jnp.where(source < 128, source >> 4, 8 + ((source >> 4) & 1))
    pick_ref[...] = jnp.where(wanted == column, 1.0 / 8192.0, 0.0).astype(BF16)
    spread = jnp.where(iota((10, 384), 0) == column[0:10], 1.0, 0.0)
    loads[4].wait()
    lit_ref[...] = dot(mask_ref[...].astype(F32), spread)
    place = iota((8, 192), 1)
    begin = 24 * iota((8, 192), 0)
    expand[...] = jnp.where((place >= begin) & (place < begin + 24), 1.0, 0.0)
    place = iota((16, 192), 1)
    entry = ((place >> 2) % 6) * 2 + (place & 1)
    for h in range(2):
        wanted = (entry == iota((16, 192), 0)) & (((place >> 1) & 1) == h)
        keep[h] = jnp.where(wanted, 1.0, 0.0)
    loads[5].wait()

    code = jnp.zeros((128, 128), jnp.int32)
    for y in range(4):
        @pl.when(jnp.logical_not(own_is_target & (chip_y == y)))
        def _(y=y):
            code_arrival(0, y).wait_recv()

    for y in range(4):
        code = code + landed[0, y].astype(jnp.int32)
    for y in range(4):
        code_arrival(1, y).wait_recv()
        code = code + landed[1, y].astype(jnp.int32)
    code = modulo_16(code)
    field_imag = sine(code)
    field_real = sine(modulo_16(code + 16384))
    real_high, real_low = split(field_real)
    imag_high, imag_low = split(field_imag)
    right = jnp.concatenate([filters[0], filters[1]], axis=1)
    across = dot(jnp.concatenate([real_high, real_low, imag_high, imag_low], axis=0), right)
    flipped_real = across[0:128, 0:128] + across[128:256, 0:128]
    flipped_imag = across[256:384, 0:128] + across[384:512, 0:128]
    turned_real = (
        across[0:128, 128:256] + across[128:256, 128:256] + dot(real_high, low_filter[...])
    )
    along_cols = (
        -16.0 * (field_real * flipped_real + field_imag * flipped_imag)
        - 2.0 * field_imag * turned_real
    )
    left = jnp.concatenate([filters[0], filters[1]], axis=0)
    down = dot(left, jnp.concatenate([real_high, real_low, imag_high, imag_low], axis=1))
    flipped_real = down[0:128, 0:128] + down[0:128, 128:256]
    flipped_imag = down[0:128, 256:384] + down[0:128, 384:512]
    turned_real = (
        down[128:256, 0:128] + down[128:256, 128:256] + dot(low_filter[...], real_high)
    )
    along_rows = (
        -16.0 * (field_real * flipped_real + field_imag * flipped_imag)
        + 2.0 * field_imag * turned_real
    )

    lane_8 = iota((8, 128), 1)
    row_8 = iota((8, 128), 0)
    sums = []
    for moment in (along_cols, along_rows):
        blocks = jnp.sum(moment.reshape(8, 16, 128), axis=1)
        shared = jnp.where(row_8 < 4, blocks[6:7, :], blocks[7:8, :])
        shared = jnp.where((lane_8 >> 5) == (row_8 & 3), shared, 0.0)
        sums.append(jnp.concatenate([blocks, shared], axis=1))
    sums = jnp.concatenate(sums, axis=0)
    high, rest = sums.astype(BF16), sums
    rest = rest - high.astype(F32)
    middle, low = split(rest)
    measured = dot(jnp.concatenate([high, middle, low], axis=0), pick_ref[...])
    measured = (measured[0:16] + measured[16:32] + measured[32:48]) * lit_ref[...]
    for star in range(STARS):
        for axis in range(2):
            slopes_ref[0, star, axis, :] = measured[axis * 8 + star, 0:10]
    lane_16 = iota((16, 256), 1)
    row_16 = iota((16, 256), 0)
    entry = (row_16 & 7) * 2 + (row_16 >> 3)
    coarse = measured[:, 128:384].astype(BF16).astype(F32)
    flat = jnp.where(((lane_16 & 15) == entry) & (entry < 12), coarse, 0.0)
    plane[in_plane] = jnp.sum(flat, axis=0, keepdims=True)

    def plane_copy(step):
        return remote(
            plane.at[in_plane],
            plane.at[in_plane],
            plane_send.at[step],
            plane_recv.at[step],
            plane_peer(step),
        )

    def plane_arrival(step):
        other = (in_plane - step + 8) % 8
        return remote(
            plane.at[in_plane],
            plane.at[other],
            plane_send.at[step],
            plane_recv.at[step],
            plane_peer(-step),
        )

    for step in range(1, 8):
        plane_copy(step).start()
    for step in range(1, 8):
        plane_arrival(step).wait_recv()

    def line_copy(step):
        return remote(
            plane, line.at[along], line_send.at[step], line_recv.at[step], line_peer(step)
        )

    def line_arrival(step):
        other = (along - step + 8) % 8
        return remote(
            plane, line.at[other], line_send.at[step], line_recv.at[step], line_peer(-step)
        )

    for step in range(1, 8):
        line_copy(step).start()
    line[along] = plane[...]

    total = jnp.zeros((32, 128), F32)
    for step in (0, 1, 7, 2, 6, 3, 5, 4):
        other = (along - step + 8) % 8
        if step:
            line_arrival(step).wait_recv()
        rows = lax.dot_general(
            line[other].reshape(8, 256)[:, 0:160],
            expand[...],
            (((0,), (0,)), ((), ())),
            preferred_element_type=F32,
        )
        for j in range(10):
            block = rows[16 * j : 16 * j + 16]
            vector = jnp.concatenate([block * keep[0], block * keep[1]], axis=0).astype(BF16)
            start = pl.multiple_of(1536 * j + 192 * other, 64)
            total = total + dot(vector, matrix[pl.ds(start, 192), :])
    own_part[...] = jnp.concatenate(
        [
            jnp.sum(total[0:16], axis=0, keepdims=True),
            jnp.sum(total[16:32], axis=0, keepdims=True),
        ],
        axis=1,
    )

    def part_copy(step):
        return remote(
            own_part, parts.at[layer], part_send.at[step], part_recv.at[step], layer_peer(step)
        )

    def part_arrival(step):
        other = (layer - step + 8) % 8
        return remote(
            own_part, parts.at[other], part_send.at[step], part_recv.at[step], layer_peer(-step)
        )

    for step in range(1, 8):
        part_copy(step).start()
    parts[layer] = own_part[...]
    for band in range(3):
        swap(band).wait_send()
    for d in range(4):
        cross(d).wait_send()
        code_copy(1, d).wait_send()

        @pl.when(jnp.logical_not(core * 4 + d == layer))
        def _(d=d):
            code_copy(0, d).wait_send()

    for step in range(1, 8):
        plane_copy(step).wait_send()
        line_copy(step).wait_send()
    for step in range(1, 8):
        part_arrival(step).wait_recv()
    total = parts[0]
    for k in range(1, 8):
        total = total + parts[k]
    commands_ref[...] = total
    for step in range(1, 8):
        part_copy(step).wait_send()


def on_device(screens, wind_shift, cone_offset, cone_weight, valid_mask, reconstructor):
    dma = pltpu.SemaphoreType.DMA
    matrix = reconstructor.reshape(3840, 2, 2, 128).transpose(0, 2, 1, 3).reshape(15360, 128)
    slopes, commands = pl.pallas_call(
        frame_kernel,
        out_shape=(
            jax.ShapeDtypeStruct((1, STARS, 2, 10), F32),
            jax.ShapeDtypeStruct((1, 256), F32),
        ),
        in_specs=[pl.BlockSpec(memory_space=pltpu.HBM)] * 6,
        out_specs=[pl.BlockSpec(memory_space=pltpu.VMEM)] * 2,
        scratch_shapes=[
            pltpu.SMEM((2, 32), jnp.int32),
            pltpu.SMEM((STARS, 32), jnp.int32),
            pltpu.SMEM((STARS, 32), F32),
            pltpu.VMEM((1, 10), jnp.int32),
            pltpu.VMEM((64, 2048), F32),
            pltpu.VMEM((64 * 11, 8, 128), F32),
            pltpu.VMEM((3, 8, 128, 128), jnp.int16),
            pltpu.VMEM((3, 4, 128, 128), jnp.int16),
            pltpu.VMEM((4, 128, 128), jnp.int16),
            pltpu.VMEM((3, 4, 128, 128), jnp.int16),
            pltpu.VMEM((2, 4, 128, 128), jnp.int16),
            pltpu.VMEM((2, 128, 128), BF16),
            pltpu.VMEM((128, 128), BF16),
            pltpu.VMEM((256, 384), BF16),
            pltpu.VMEM((1, 384), F32),
            pltpu.VMEM((8, 192), F32),
            pltpu.VMEM((2, 16, 192), F32),
            pltpu.VMEM((8, 1, 256), F32),
            pltpu.VMEM((8, 8, 1, 256), F32),
            pltpu.VMEM((15360, 128), BF16),
            pltpu.VMEM((1, 256), F32),
            pltpu.VMEM((8, 1, 256), F32),
            dma((6,)),
            dma((3,)),
            dma((3,)),
            dma((4,)),
            dma((4,)),
            dma((2, 4)),
            dma((2, 4)),
            dma((8,)),
            dma((8,)),
            dma((8,)),
            dma((8,)),
            dma((8,)),
            dma((8,)),
        ],
        compiler_params=pltpu.CompilerParams(
            collective_id=0, has_side_effects=True, vmem_limit_bytes=66_900_000
        ),
        name="frame",
    )(
        wind_shift.T,
        cone_offset,
        cone_weight,
        valid_mask,
        screens.reshape(64, 2048),
        matrix,
    )
    return slopes, commands.reshape(-1)


def solution(mesh):
    placed = (
        P("layer", "tile", None),
        P(),
        P(),
        P(),
        P("tile", "layer"),
        P("layer", None, None, None, "tile"),
    )
    return jax.shard_map(
        on_device,
        mesh=mesh,
        in_specs=placed,
        out_specs=(P("tile", None, None, "layer"), P("tile")),
        check_vma=False,
    )
```

```python
import math

import jax
import jax.numpy as jnp
from jax import lax
from jax.experimental import pallas as pl
from jax.experimental.pallas import tpu as pltpu
from jax.sharding import PartitionSpec as P

STARS = 6
SPAN = 160
TILES = 64
UNIT = 2.0 * math.pi / 65536.0
MESH = pl.DeviceIdType.MESH
F32 = jnp.float32
BF16 = jnp.bfloat16
SINE = (
    1.5707962900208665,
    -0.6459633598429161,
    0.07968848044711395,
    -0.0046722277849454265,
    0.00015082049685476598,
)


def modulo_16(q):
    return ((q + 32768) & 65535) - 32768


def iota(shape, axis):
    return lax.broadcasted_iota(jnp.int32, shape, axis)


def split(x):
    high = x.astype(BF16)
    return high, (x - high.astype(F32)).astype(BF16)


def dot(a, b):
    return jnp.dot(a, b, preferred_element_type=F32)


def sine(q):
    q = jnp.where(q > 16384, 32768 - q, jnp.where(q < -16384, -32768 - q, q))
    x = q.astype(F32) * (1.0 / 16384.0)
    square = x * x
    value = SINE[4]
    for coefficient in SINE[3::-1]:
        value = value * square + coefficient
    return value * x


def filter_tables():
    row = iota((128, 128), 0)
    col = iota((128, 128), 1)
    gap = row - col
    same = (row >> 4) == (col >> 4)
    sign = jnp.where((gap & 1) == 0, 1.0, -1.0)
    angle = gap.astype(F32) * (math.pi / 32.0)
    inside = jnp.where(same & (gap != 0), angle, math.pi / 2.0)
    cotangent = jnp.cos(inside) / jnp.sin(inside)
    flips = jnp.where(same, sign, 0.0)
    odd = jnp.where(same & (gap != 0), -16.0 * sign * cotangent, 0.0)
    return flips, odd


def frame_kernel(
    wind_hbm,
    offset_hbm,
    weight_hbm,
    mask_hbm,
    screens_hbm,
    matrix_hbm,
    slopes_ref,
    commands_ref,
    wind,
    cone_offset,
    cone_weight,
    mask_ref,
    held,
    placed,
    partial,
    swapped,
    crossed,
    coded,
    landed,
    filters,
    low_filter,
    pick_ref,
    lit_ref,
    expand,
    keep,
    plane,
    line,
    matrix,
    own_part,
    parts,
    load_sem,
    swap_send,
    swap_recv,
    cross_send,
    cross_recv,
    code_send,
    code_recv,
    plane_send,
    plane_recv,
    line_send,
    line_recv,
    part_send,
    part_recv,
):
    tile = lax.axis_index("tile")
    layer = lax.axis_index("layer")
    chip_y = layer // 2
    core = layer % 2
    half = layer // 4
    in_plane = tile % 8
    along = tile // 8

    def at(tile_index, layer_index):
        return (tile_index, layer_index)

    partner = at(tile, layer + 1 - 2 * core)
    side = tile % 2
    near_tile = tile + 1 - 2 * side
    near_band = 2 - 2 * side
    far_band = 2 * side
    onward = at((tile + 4 * side - 2 + TILES) % TILES, layer)
    backward = at((tile - 4 * side + 2 + TILES) % TILES, layer)

    def code_target(near, d):
        return at(near_tile if near else tile, core * 4 + d)

    def code_source(near, y):
        return at(near_tile if near else tile, y * 2 + half)

    def plane_peer(step):
        return at(along * 8 + (in_plane + step + 8) % 8, layer)

    def line_peer(step):
        return at(((along + step + 8) % 8) * 8 + in_plane, layer)

    def layer_peer(step):
        return at(tile, (layer + step + 8) % 8)

    barrier = pltpu.get_barrier_semaphore()
    loads = [
        pltpu.make_async_copy(source, target, load_sem.at[k])
        for k, (source, target) in enumerate(
            (
                (screens_hbm, held),
                (wind_hbm, wind),
                (offset_hbm, cone_offset),
                (weight_hbm, cone_weight),
                (mask_hbm, mask_ref),
                (matrix_hbm, matrix),
            )
        )
    ]
    for load in loads:
        load.start()

    def greet(where):
        pl.semaphore_signal(barrier, inc=1, device_id=where, device_id_type=MESH)

    greet(partner)
    greet(backward)
    own_is_target = half == core
    for y in range(4):
        greet(code_source(True, y))

        @pl.when(jnp.logical_not(own_is_target & (chip_y == y)))
        def _(y=y):
            greet(code_source(False, y))

    for step in range(1, 8):
        greet(plane_peer(-step))
        greet(line_peer(-step))
        greet(layer_peer(-step))

    zeros = jnp.zeros((5, 8, 128), F32)

    def clear(k, carry):
        placed[pl.ds(11 * k, 5)] = zeros
        placed[pl.ds(11 * k + 8, 3)] = zeros[0:3]
        return carry

    lax.fori_loop(0, 64, clear, 0, unroll=8)
    for load in loads[:4]:
        load.wait()
    row = iota((8, 128), 0)
    for slot in range(4):
        down = (wind[0, layer * 4 + slot] + 16) & 7
        early = row < down
        for m in range(16):
            columns = slice(128 * m, 128 * m + 128)
            upper = pltpu.roll(held[16 * slot : 16 * slot + 8, columns], down, axis=0)
            lower = pltpu.roll(held[16 * slot + 8 : 16 * slot + 16, columns], down, axis=0)
            group = 11 * (16 * slot + m) + 5
            placed[group] = jnp.where(early, 0.0, upper)
            placed[group + 1] = jnp.where(early, upper, lower)
            placed[group + 2] = jnp.where(early, lower, 0.0)

    lane = iota((16, 128), 1)

    def add_layers(band):
        tails = [None] * 8
        for star in range(STARS):
            total = [None] * 10
            for slot in range(4):
                which = layer * 4 + slot
                beginning = wind[1, which] + cone_offset[star, which]
                weight = cone_weight[star, which]
                column = lax.shift_right_logical(beginning, 7) + 16 * slot
                first = 11 * column + 5 - lax.shift_right_logical(wind[0, which] + 16, 3)
                first = first + 2 * band
                turn = beginning & 127
                roll_by = (128 - turn) & 127
                stay = lane < 128 - turn

                def turned(m, first=first, roll_by=roll_by):
                    window = placed[pl.ds(first + 11 * m, 2)].reshape(16, 128)
                    return pltpu.roll(window, roll_by, axis=1)

                before = turned(0)
                for m in range(10):
                    after = turned(m + 1)
                    term = weight * jnp.where(stay, before, after)
                    total[m] = term if slot == 0 else total[m] + term
                    before = after
            code = [jnp.round(part * (1.0 / UNIT)).astype(jnp.int32) for part in total]
            for block in range(8):
                tile_at, start = (block * SPAN) // 128, (block * SPAN) % 128
                main = code[tile_at]
                if start > 0:
                    main = jnp.where(
                        lane < 128 - start,
                        pltpu.roll(main, 128 - start, axis=1),
                        pltpu.roll(code[tile_at + 1], 128 - start, axis=1),
                    )
                place = 32 * (star % 4)
                tail = code[tile_at + 1]
                if place != start:
                    tail = pltpu.roll(tail, (place - start) % 128, axis=1)
                tail = jnp.where((lane >= place) & (lane < place + 32), tail, 0)
                tails[block] = tail if star % 4 == 0 else tails[block] + tail
                partial[band, block, 16 * star : 16 * star + 16, :] = main.astype(jnp.int16)
                if star in (3, 5):
                    at_row = 96 + 16 * (star // 4)
                    partial[band, block, at_row : at_row + 16, :] = tails[block].astype(jnp.int16)

    def remote(source, target, send, recv, where):
        return pltpu.make_async_remote_copy(
            src_ref=source,
            dst_ref=target,
            send_sem=send,
            recv_sem=recv,
            device_id=where,
            device_id_type=MESH,
        )

    def swap(band):
        return remote(
            partial.at[band, pl.ds((1 - core) * 4, 4)],
            swapped.at[band],
            swap_send.at[band],
            swap_recv.at[band],
            partner,
        )

    def cross(d):
        return remote(
            coded.at[far_band, d], crossed.at[d], cross_send.at[d], cross_recv.at[d], onward
        )

    def code_copy(near, d):
        return remote(
            coded.at[near_band if near else 1, d],
            landed.at[near, chip_y],
            code_send.at[near, d],
            code_recv.at[near, chip_y],
            code_target(near, d),
        )

    def code_arrival(near, y):
        return remote(
            coded.at[near_band if near else 1, 0],
            landed.at[near, y],
            code_send.at[near, 0],
            code_recv.at[near, y],
            code_source(near, y),
        )

    def both(band, d):
        own = partial[band, core * 4 + d].astype(jnp.int32)
        return own + swapped[band, d].astype(jnp.int32)

    add_layers(far_band)
    pl.semaphore_wait(barrier, 31 - own_is_target.astype(jnp.int32))
    swap(far_band).start()
    add_layers(1)
    swap(1).start()
    swap(far_band).wait_recv()
    for d in range(4):
        coded[far_band, d] = both(far_band, d).astype(jnp.int16)
        cross(d).start()
    add_layers(near_band)
    swap(near_band).start()
    swap(1).wait_recv()
    for d in range(4):
        coded[1, d] = both(1, d).astype(jnp.int16)
    for d in range(4):
        is_self = core * 4 + d == layer

        @pl.when(jnp.logical_not(is_self))
        def _(d=d):
            code_copy(0, d).start()

        @pl.when(is_self)
        def _(d=d):
            landed[0, chip_y] = coded[1, d]

    swap(near_band).wait_recv()
    for d in range(4):
        cross(d).wait_recv()
        total = both(near_band, d) + crossed[d].astype(jnp.int32)
        coded[near_band, d] = total.astype(jnp.int16)
        code_copy(1, d).start()

    flips, odd = filter_tables()
    odd_high, odd_low = split(odd)
    filters[0] = flips.astype(BF16)
    filters[1] = odd_high
    low_filter[...] = odd_low
    column = iota((256, 384), 1)
    column = jnp.where(column < 128, column, (column - 128) >> 4)
    source = iota((256, 384), 0)
    wanted = jnp.where(source < 128, source >> 4, 8 + ((source >> 4) & 1))
    pick_ref[...] = jnp.where(wanted == column, 1.0 / 8192.0, 0.0).astype(BF16)
    spread = jnp.where(iota((10, 384), 0) == column[0:10], 1.0, 0.0)
    loads[4].wait()
    lit_ref[...] = dot(mask_ref[...].astype(F32), spread)
    place = iota((8, 192), 1)
    begin = 24 * iota((8, 192), 0)
    expand[...] = jnp.where((place >= begin) & (place < begin + 24), 1.0, 0.0)
    place = iota((16, 192), 1)
    entry = ((place >> 2) % 6) * 2 + (place & 1)
    for h in range(2):
        wanted = (entry == iota((16, 192), 0)) & (((place >> 1) & 1) == h)
        keep[h] = jnp.where(wanted, 1.0, 0.0)
    loads[5].wait()

    code = jnp.zeros((128, 128), jnp.int32)
    for y in range(4):
        @pl.when(jnp.logical_not(own_is_target & (chip_y == y)))
        def _(y=y):
            code_arrival(0, y).wait_recv()

    for y in range(4):
        code = code + landed[0, y].astype(jnp.int32)
    for y in range(4):
        code_arrival(1, y).wait_recv()
        code = code + landed[1, y].astype(jnp.int32)
    code = modulo_16(code)
    field_imag = sine(code)
    field_real = sine(modulo_16(code + 16384))
    real_high, real_low = split(field_real)
    imag_high, imag_low = split(field_imag)
    right = jnp.concatenate([filters[0], filters[1]], axis=1)
    across = dot(jnp.concatenate([real_high, real_low, imag_high, imag_low], axis=0), right)
    flipped_real = across[0:128, 0:128] + across[128:256, 0:128]
    flipped_imag = across[256:384, 0:128] + across[384:512, 0:128]
    turned_real = (
        across[0:128, 128:256] + across[128:256, 128:256] + dot(real_high, low_filter[...])
    )
    along_cols = (
        -16.0 * (field_real * flipped_real + field_imag * flipped_imag)
        - 2.0 * field_imag * turned_real
    )
    left = jnp.concatenate([filters[0], filters[1]], axis=0)
    down = dot(left, jnp.concatenate([real_high, real_low, imag_high, imag_low], axis=1))
    flipped_real = down[0:128, 0:128] + down[0:128, 128:256]
    flipped_imag = down[0:128, 256:384] + down[0:128, 384:512]
    turned_real = (
        down[128:256, 0:128] + down[128:256, 128:256] + dot(low_filter[...], real_high)
    )
    along_rows = (
        -16.0 * (field_real * flipped_real + field_imag * flipped_imag)
        + 2.0 * field_imag * turned_real
    )

    lane_8 = iota((8, 128), 1)
    row_8 = iota((8, 128), 0)
    sums = []
    for moment in (along_cols, along_rows):
        blocks = jnp.sum(moment.reshape(8, 16, 128), axis=1)
        shared = jnp.where(row_8 < 4, blocks[6:7, :], blocks[7:8, :])
        shared = jnp.where((lane_8 >> 5) == (row_8 & 3), shared, 0.0)
        sums.append(jnp.concatenate([blocks, shared], axis=1))
    sums = jnp.concatenate(sums, axis=0)
    high, rest = sums.astype(BF16), sums
    rest = rest - high.astype(F32)
    middle, low = split(rest)
    measured = dot(jnp.concatenate([high, middle, low], axis=0), pick_ref[...])
    measured = (measured[0:16] + measured[16:32] + measured[32:48]) * lit_ref[...]
    for star in range(STARS):
        for axis in range(2):
            slopes_ref[0, star, axis, :] = measured[axis * 8 + star, 0:10]
    lane_16 = iota((16, 256), 1)
    row_16 = iota((16, 256), 0)
    entry = (row_16 & 7) * 2 + (row_16 >> 3)
    coarse = measured[:, 128:384].astype(BF16).astype(F32)
    flat = jnp.where(((lane_16 & 15) == entry) & (entry < 12), coarse, 0.0)
    plane[in_plane] = jnp.sum(flat, axis=0, keepdims=True)

    def plane_copy(step):
        return remote(
            plane.at[in_plane],
            plane.at[in_plane],
            plane_send.at[step],
            plane_recv.at[step],
            plane_peer(step),
        )

    def plane_arrival(step):
        other = (in_plane - step + 8) % 8
        return remote(
            plane.at[in_plane],
            plane.at[other],
            plane_send.at[step],
            plane_recv.at[step],
            plane_peer(-step),
        )

    for step in range(1, 8):
        plane_copy(step).start()
    for step in range(1, 8):
        plane_arrival(step).wait_recv()

    def line_copy(step):
        return remote(
            plane, line.at[along], line_send.at[step], line_recv.at[step], line_peer(step)
        )

    def line_arrival(step):
        other = (along - step + 8) % 8
        return remote(
            plane, line.at[other], line_send.at[step], line_recv.at[step], line_peer(-step)
        )

    for step in range(1, 8):
        line_copy(step).start()
    line[along] = plane[...]

    total = jnp.zeros((32, 128), F32)
    for step in (0, 1, 7, 2, 6, 3, 5, 4):
        other = (along - step + 8) % 8
        if step:
            line_arrival(step).wait_recv()
        rows = lax.dot_general(
            line[other].reshape(8, 256)[:, 0:160],
            expand[...],
            (((0,), (0,)), ((), ())),
            preferred_element_type=F32,
        )
        for j in range(10):
            block = rows[16 * j : 16 * j + 16]
            vector = jnp.concatenate([block * keep[0], block * keep[1]], axis=0).astype(BF16)
            start = pl.multiple_of(1536 * j + 192 * other, 64)
            total = total + dot(vector, matrix[pl.ds(start, 192), :])
    own_part[...] = jnp.concatenate(
        [
            jnp.sum(total[0:16], axis=0, keepdims=True),
            jnp.sum(total[16:32], axis=0, keepdims=True),
        ],
        axis=1,
    )

    def part_copy(step):
        return remote(
            own_part, parts.at[layer], part_send.at[step], part_recv.at[step], layer_peer(step)
        )

    def part_arrival(step):
        other = (layer - step + 8) % 8
        return remote(
            own_part, parts.at[other], part_send.at[step], part_recv.at[step], layer_peer(-step)
        )

    for step in range(1, 8):
        part_copy(step).start()
    parts[layer] = own_part[...]
    for band in range(3):
        swap(band).wait_send()
    for d in range(4):
        cross(d).wait_send()
        code_copy(1, d).wait_send()

        @pl.when(jnp.logical_not(core * 4 + d == layer))
        def _(d=d):
            code_copy(0, d).wait_send()

    for step in range(1, 8):
        plane_copy(step).wait_send()
        line_copy(step).wait_send()
    for step in range(1, 8):
        part_arrival(step).wait_recv()
    total = parts[0]
    for k in range(1, 8):
        total = total + parts[k]
    commands_ref[...] = total
    for step in range(1, 8):
        part_copy(step).wait_send()


def publish_kernel(slopes_in, commands_in, slopes_ref, commands_ref, sem):
    copies = [
        pltpu.make_async_copy(slopes_in, slopes_ref, sem.at[0]),
        pltpu.make_async_copy(commands_in, commands_ref, sem.at[1]),
    ]
    for copy in copies:
        copy.start()
    for copy in copies:
        copy.wait()


def publish(slopes, commands):
    return pl.pallas_call(
        publish_kernel,
        out_shape=(
            jax.ShapeDtypeStruct(slopes.shape, F32),
            jax.ShapeDtypeStruct(commands.shape, F32),
        ),
        in_specs=[pl.BlockSpec(memory_space=pltpu.HBM)] * 2,
        out_specs=[pl.BlockSpec(memory_space=pltpu.HBM)] * 2,
        scratch_shapes=[pltpu.SemaphoreType.DMA((2,))],
        compiler_params=pltpu.CompilerParams(vmem_limit_bytes=66_900_000),
        name="publish",
    )(slopes, commands)


def on_device(screens, wind_shift, cone_offset, cone_weight, valid_mask, reconstructor):
    dma = pltpu.SemaphoreType.DMA
    matrix = reconstructor.reshape(3840, 2, 2, 128).transpose(0, 2, 1, 3).reshape(15360, 128)
    slopes, commands = pl.pallas_call(
        frame_kernel,
        out_shape=(
            jax.ShapeDtypeStruct((1, STARS, 2, 10), F32),
            jax.ShapeDtypeStruct((1, 256), F32),
        ),
        in_specs=[pl.BlockSpec(memory_space=pltpu.HBM)] * 6,
        out_specs=[pl.BlockSpec(memory_space=pltpu.VMEM)] * 2,
        scratch_shapes=[
            pltpu.SMEM((2, 32), jnp.int32),
            pltpu.SMEM((STARS, 32), jnp.int32),
            pltpu.SMEM((STARS, 32), F32),
            pltpu.VMEM((1, 10), jnp.int32),
            pltpu.VMEM((64, 2048), F32),
            pltpu.VMEM((64 * 11, 8, 128), F32),
            pltpu.VMEM((3, 8, 128, 128), jnp.int16),
            pltpu.VMEM((3, 4, 128, 128), jnp.int16),
            pltpu.VMEM((4, 128, 128), jnp.int16),
            pltpu.VMEM((3, 4, 128, 128), jnp.int16),
            pltpu.VMEM((2, 4, 128, 128), jnp.int16),
            pltpu.VMEM((2, 128, 128), BF16),
            pltpu.VMEM((128, 128), BF16),
            pltpu.VMEM((256, 384), BF16),
            pltpu.VMEM((1, 384), F32),
            pltpu.VMEM((8, 192), F32),
            pltpu.VMEM((2, 16, 192), F32),
            pltpu.VMEM((8, 1, 256), F32),
            pltpu.VMEM((8, 8, 1, 256), F32),
            pltpu.VMEM((15360, 128), BF16),
            pltpu.VMEM((1, 256), F32),
            pltpu.VMEM((8, 1, 256), F32),
            dma((6,)),
            dma((3,)),
            dma((3,)),
            dma((4,)),
            dma((4,)),
            dma((2, 4)),
            dma((2, 4)),
            dma((8,)),
            dma((8,)),
            dma((8,)),
            dma((8,)),
            dma((8,)),
            dma((8,)),
        ],
        compiler_params=pltpu.CompilerParams(
            collective_id=0, has_side_effects=True, vmem_limit_bytes=66_900_000
        ),
        name="frame",
    )(
        wind_shift.T,
        cone_offset,
        cone_weight,
        valid_mask,
        screens.reshape(64, 2048),
        matrix,
    )
    slopes, commands = publish(slopes, commands)
    return slopes, commands.reshape(-1)


def solution(mesh):
    placed = (
        P("layer", "tile", None),
        P(),
        P(),
        P(),
        P("tile", "layer"),
        P("layer", None, None, None, "tile"),
    )
    return jax.shard_map(
        on_device,
        mesh=mesh,
        in_specs=placed,
        out_specs=(P("tile", None, None, "layer"), P("tile")),
        check_vma=False,
    )
```

```python
import math

import jax
import jax.numpy as jnp
from jax import lax
from jax.experimental import pallas as pl
from jax.experimental.pallas import tpu as pltpu
from jax.sharding import PartitionSpec as P

STARS = 6
SPAN = 160
TILES = 64
UNIT = 2.0 * math.pi / 65536.0
MESH = pl.DeviceIdType.MESH
F32 = jnp.float32
BF16 = jnp.bfloat16
SINE = (
    1.5707962900208665,
    -0.6459633598429161,
    0.07968848044711395,
    -0.0046722277849454265,
    0.00015082049685476598,
)


def modulo_16(q):
    return ((q + 32768) & 65535) - 32768


def iota(shape, axis):
    return lax.broadcasted_iota(jnp.int32, shape, axis)


def split(x):
    high = x.astype(BF16)
    return high, (x - high.astype(F32)).astype(BF16)


def dot(a, b):
    return jnp.dot(a, b, preferred_element_type=F32)


def sine(q):
    q = jnp.where(q > 16384, 32768 - q, jnp.where(q < -16384, -32768 - q, q))
    x = q.astype(F32) * (1.0 / 16384.0)
    square = x * x
    value = SINE[4]
    for coefficient in SINE[3::-1]:
        value = value * square + coefficient
    return value * x


def filter_tables():
    row = iota((128, 128), 0)
    col = iota((128, 128), 1)
    gap = row - col
    same = (row >> 4) == (col >> 4)
    sign = jnp.where((gap & 1) == 0, 1.0, -1.0)
    angle = gap.astype(F32) * (math.pi / 32.0)
    inside = jnp.where(same & (gap != 0), angle, math.pi / 2.0)
    cotangent = jnp.cos(inside) / jnp.sin(inside)
    flips = jnp.where(same, sign, 0.0)
    odd = jnp.where(same & (gap != 0), -16.0 * sign * cotangent, 0.0)
    return flips, odd


def frame_kernel(
    wind_hbm,
    offset_hbm,
    weight_hbm,
    mask_hbm,
    screens_hbm,
    matrix_hbm,
    slopes_ref,
    commands_ref,
    wind,
    cone_offset,
    cone_weight,
    mask_ref,
    held,
    placed,
    partial,
    swapped,
    crossed,
    coded,
    landed,
    filters,
    low_filter,
    pick_ref,
    lit_ref,
    expand,
    keep,
    plane,
    line,
    matrix,
    own_part,
    parts,
    load_sem,
    swap_send,
    swap_recv,
    cross_send,
    cross_recv,
    code_send,
    code_recv,
    plane_send,
    plane_recv,
    line_send,
    line_recv,
    part_send,
    part_recv,
):
    tile = lax.axis_index("tile")
    layer = lax.axis_index("layer")
    chip_y = layer // 2
    core = layer % 2
    half = layer // 4
    in_plane = tile % 8
    along = tile // 8

    def at(tile_index, layer_index):
        return (tile_index, layer_index)

    partner = at(tile, layer + 1 - 2 * core)
    side = tile % 2
    near_tile = tile + 1 - 2 * side
    near_band = 2 - 2 * side
    far_band = 2 * side
    onward = at((tile + 4 * side - 2 + TILES) % TILES, layer)
    backward = at((tile - 4 * side + 2 + TILES) % TILES, layer)

    def code_target(near, d):
        return at(near_tile if near else tile, core * 4 + d)

    def code_source(near, y):
        return at(near_tile if near else tile, y * 2 + half)

    def plane_peer(step):
        return at(along * 8 + (in_plane + step + 8) % 8, layer)

    def line_peer(step):
        return at(((along + step + 8) % 8) * 8 + in_plane, layer)

    def layer_peer(step):
        return at(tile, (layer + step + 8) % 8)

    barrier = pltpu.get_barrier_semaphore()
    loads = [
        pltpu.make_async_copy(source, target, load_sem.at[k])
        for k, (source, target) in enumerate(
            (
                (screens_hbm, held),
                (wind_hbm, wind),
                (offset_hbm, cone_offset),
                (weight_hbm, cone_weight),
                (mask_hbm, mask_ref),
                (matrix_hbm, matrix),
            )
        )
    ]
    for load in loads:
        load.start()

    def greet(where):
        pl.semaphore_signal(barrier, inc=1, device_id=where, device_id_type=MESH)

    own_is_target = half == core
    for step in (4, 3, 5, 2, 6, 1, 7):
        greet(layer_peer(step))
    for y in range(4):
        greet(code_source(True, y))
    for step in (4, 3, 5, 2, 6, 1, 7):
        greet(line_peer(step))
    for step in range(1, 8):
        greet(plane_peer(step))
    greet(backward)

    zeros = jnp.zeros((5, 8, 128), F32)

    def clear(k, carry):
        placed[pl.ds(11 * k, 5)] = zeros
        placed[pl.ds(11 * k + 8, 3)] = zeros[0:3]
        return carry

    lax.fori_loop(0, 64, clear, 0, unroll=8)
    for load in loads[:4]:
        load.wait()
    row = iota((8, 128), 0)
    for slot in range(4):
        down = (wind[0, layer * 4 + slot] + 16) & 7
        early = row < down
        for m in range(16):
            columns = slice(128 * m, 128 * m + 128)
            upper = pltpu.roll(held[16 * slot : 16 * slot + 8, columns], down, axis=0)
            lower = pltpu.roll(held[16 * slot + 8 : 16 * slot + 16, columns], down, axis=0)
            group = 11 * (16 * slot + m) + 5
            placed[group] = jnp.where(early, 0.0, upper)
            placed[group + 1] = jnp.where(early, upper, lower)
            placed[group + 2] = jnp.where(early, lower, 0.0)

    lane = iota((16, 128), 1)

    def add_layers(band):
        tails = [None] * 8
        for star in range(STARS):
            total = [None] * 10
            for slot in range(4):
                which = layer * 4 + slot
                beginning = wind[1, which] + cone_offset[star, which]
                weight = cone_weight[star, which]
                column = lax.shift_right_logical(beginning, 7) + 16 * slot
                first = 11 * column + 5 - lax.shift_right_logical(wind[0, which] + 16, 3)
                first = first + 2 * band
                turn = beginning & 127
                roll_by = (128 - turn) & 127
                stay = lane < 128 - turn

                def turned(m, first=first, roll_by=roll_by):
                    window = placed[pl.ds(first + 11 * m, 2)].reshape(16, 128)
                    return pltpu.roll(window, roll_by, axis=1)

                before = turned(0)
                for m in range(10):
                    after = turned(m + 1)
                    term = weight * jnp.where(stay, before, after)
                    total[m] = term if slot == 0 else total[m] + term
                    before = after
            code = [jnp.round(part * (1.0 / UNIT)).astype(jnp.int32) for part in total]
            for block in range(8):
                tile_at, start = (block * SPAN) // 128, (block * SPAN) % 128
                main = code[tile_at]
                if start > 0:
                    main = jnp.where(
                        lane < 128 - start,
                        pltpu.roll(main, 128 - start, axis=1),
                        pltpu.roll(code[tile_at + 1], 128 - start, axis=1),
                    )
                place = 32 * (star % 4)
                tail = code[tile_at + 1]
                if place != start:
                    tail = pltpu.roll(tail, (place - start) % 128, axis=1)
                tail = jnp.where((lane >= place) & (lane < place + 32), tail, 0)
                tails[block] = tail if star % 4 == 0 else tails[block] + tail
                partial[band, block, 16 * star : 16 * star + 16, :] = main.astype(jnp.int16)
                if star in (3, 5):
                    at_row = 96 + 16 * (star // 4)
                    partial[band, block, at_row : at_row + 16, :] = tails[block].astype(jnp.int16)

    def remote(source, target, send, recv, where):
        return pltpu.make_async_remote_copy(
            src_ref=source,
            dst_ref=target,
            send_sem=send,
            recv_sem=recv,
            device_id=where,
            device_id_type=MESH,
        )

    def swap(band):
        return remote(
            partial.at[band, pl.ds((1 - core) * 4, 4)],
            swapped.at[band],
            swap_send.at[band],
            swap_recv.at[band],
            partner,
        )

    def cross(d):
        return remote(
            coded.at[far_band, d], crossed.at[d], cross_send.at[d], cross_recv.at[d], onward
        )

    def code_copy(near, d):
        return remote(
            coded.at[near_band if near else 1, d],
            landed.at[near, chip_y],
            code_send.at[near, d],
            code_recv.at[near, chip_y],
            code_target(near, d),
        )

    def code_arrival(near, y):
        return remote(
            coded.at[near_band if near else 1, 0],
            landed.at[near, y],
            code_send.at[near, 0],
            code_recv.at[near, y],
            code_source(near, y),
        )

    def both(band, d):
        own = partial[band, core * 4 + d].astype(jnp.int32)
        return own + swapped[band, d].astype(jnp.int32)

    add_layers(far_band)
    add_layers(1)
    pl.semaphore_wait(barrier, 26)
    swap(far_band).start()
    swap(1).start()
    add_layers(near_band)
    swap(near_band).start()
    swap(far_band).wait_recv()
    for d in range(4):
        coded[far_band, d] = both(far_band, d).astype(jnp.int16)
        cross(d).start()
    swap(1).wait_recv()
    for d in range(4):
        coded[1, d] = both(1, d).astype(jnp.int16)
    for d in range(4):
        is_self = core * 4 + d == layer

        @pl.when(jnp.logical_not(is_self))
        def _(d=d):
            code_copy(0, d).start()

        @pl.when(is_self)
        def _(d=d):
            landed[0, chip_y] = coded[1, d]

    swap(near_band).wait_recv()
    for d in range(4):
        cross(d).wait_recv()
        total = both(near_band, d) + crossed[d].astype(jnp.int32)
        coded[near_band, d] = total.astype(jnp.int16)
        code_copy(1, d).start()

    flips, odd = filter_tables()
    odd_high, odd_low = split(odd)
    filters[0] = flips.astype(BF16)
    filters[1] = odd_high
    low_filter[...] = odd_low
    column = iota((256, 384), 1)
    column = jnp.where(column < 128, column, (column - 128) >> 4)
    source = iota((256, 384), 0)
    wanted = jnp.where(source < 128, source >> 4, 8 + ((source >> 4) & 1))
    pick_ref[...] = jnp.where(wanted == column, 1.0 / 8192.0, 0.0).astype(BF16)
    spread = jnp.where(iota((10, 384), 0) == column[0:10], 1.0, 0.0)
    loads[4].wait()
    lit_ref[...] = dot(mask_ref[...].astype(F32), spread)
    place = iota((8, 192), 1)
    begin = 24 * iota((8, 192), 0)
    expand[...] = jnp.where((place >= begin) & (place < begin + 24), 1.0, 0.0)
    place = iota((16, 192), 1)
    entry = ((place >> 2) % 6) * 2 + (place & 1)
    for h in range(2):
        wanted = (entry == iota((16, 192), 0)) & (((place >> 1) & 1) == h)
        keep[h] = jnp.where(wanted, 1.0, 0.0)
    loads[5].wait()

    code = jnp.zeros((128, 128), jnp.int32)
    for y in range(4):
        @pl.when(jnp.logical_not(own_is_target & (chip_y == y)))
        def _(y=y):
            code_arrival(0, y).wait_recv()

    for y in range(4):
        code = code + landed[0, y].astype(jnp.int32)
    for y in range(4):
        code_arrival(1, y).wait_recv()
        code = code + landed[1, y].astype(jnp.int32)
    code = modulo_16(code)
    field_imag = sine(code)
    field_real = sine(modulo_16(code + 16384))
    real_high, real_low = split(field_real)
    imag_high, imag_low = split(field_imag)
    right = jnp.concatenate([filters[0], filters[1]], axis=1)
    across = dot(jnp.concatenate([real_high, real_low, imag_high, imag_low], axis=0), right)
    flipped_real = across[0:128, 0:128] + across[128:256, 0:128]
    flipped_imag = across[256:384, 0:128] + across[384:512, 0:128]
    turned_real = (
        across[0:128, 128:256] + across[128:256, 128:256] + dot(real_high, low_filter[...])
    )
    along_cols = (
        -16.0 * (field_real * flipped_real + field_imag * flipped_imag)
        - 2.0 * field_imag * turned_real
    )
    left = jnp.concatenate([filters[0], filters[1]], axis=0)
    down = dot(left, jnp.concatenate([real_high, real_low, imag_high, imag_low], axis=1))
    flipped_real = down[0:128, 0:128] + down[0:128, 128:256]
    flipped_imag = down[0:128, 256:384] + down[0:128, 384:512]
    turned_real = (
        down[128:256, 0:128] + down[128:256, 128:256] + dot(low_filter[...], real_high)
    )
    along_rows = (
        -16.0 * (field_real * flipped_real + field_imag * flipped_imag)
        + 2.0 * field_imag * turned_real
    )

    lane_8 = iota((8, 128), 1)
    row_8 = iota((8, 128), 0)
    sums = []
    for moment in (along_cols, along_rows):
        blocks = jnp.sum(moment.reshape(8, 16, 128), axis=1)
        shared = jnp.where(row_8 < 4, blocks[6:7, :], blocks[7:8, :])
        shared = jnp.where((lane_8 >> 5) == (row_8 & 3), shared, 0.0)
        sums.append(jnp.concatenate([blocks, shared], axis=1))
    sums = jnp.concatenate(sums, axis=0)
    high, rest = sums.astype(BF16), sums
    rest = rest - high.astype(F32)
    middle, low = split(rest)
    measured = dot(jnp.concatenate([high, middle, low], axis=0), pick_ref[...])
    measured = (measured[0:16] + measured[16:32] + measured[32:48]) * lit_ref[...]
    for star in range(STARS):
        for axis in range(2):
            slopes_ref[0, star, axis, :] = measured[axis * 8 + star, 0:10]
    lane_16 = iota((16, 256), 1)
    row_16 = iota((16, 256), 0)
    entry = (row_16 & 7) * 2 + (row_16 >> 3)
    coarse = measured[:, 128:384].astype(BF16).astype(F32)
    flat = jnp.where(((lane_16 & 15) == entry) & (entry < 12), coarse, 0.0)
    plane[in_plane] = jnp.sum(flat, axis=0, keepdims=True)

    def plane_copy(step):
        return remote(
            plane.at[in_plane],
            plane.at[in_plane],
            plane_send.at[step],
            plane_recv.at[step],
            plane_peer(step),
        )

    def plane_arrival(step):
        other = (in_plane - step + 8) % 8
        return remote(
            plane.at[in_plane],
            plane.at[other],
            plane_send.at[step],
            plane_recv.at[step],
            plane_peer(-step),
        )

    for step in range(1, 8):
        plane_copy(step).start()
    for step in range(1, 8):
        plane_arrival(step).wait_recv()

    def line_copy(step):
        return remote(
            plane, line.at[along], line_send.at[step], line_recv.at[step], line_peer(step)
        )

    def line_arrival(step):
        other = (along - step + 8) % 8
        return remote(
            plane, line.at[other], line_send.at[step], line_recv.at[step], line_peer(-step)
        )

    for step in range(1, 8):
        line_copy(step).start()
    line[along] = plane[...]

    total = jnp.zeros((32, 128), F32)
    for other in range(8):
        @pl.when(along != other)
        def _(other=other):
            line_arrival((along - other + 8) % 8).wait_recv()

        rows = lax.dot_general(
            line[other].reshape(8, 256)[:, 0:160],
            expand[...],
            (((0,), (0,)), ((), ())),
            preferred_element_type=F32,
        )
        for j in range(10):
            block = rows[16 * j : 16 * j + 16]
            vector = jnp.concatenate([block * keep[0], block * keep[1]], axis=0).astype(BF16)
            start = 1536 * j + 192 * other
            total = total + dot(vector, matrix[start : start + 192, :])
    own_part[...] = jnp.concatenate(
        [
            jnp.sum(total[0:16], axis=0, keepdims=True),
            jnp.sum(total[16:32], axis=0, keepdims=True),
        ],
        axis=1,
    )

    def part_copy(step):
        return remote(
            own_part, parts.at[layer], part_send.at[step], part_recv.at[step], layer_peer(step)
        )

    def part_arrival(step):
        other = (layer - step + 8) % 8
        return remote(
            own_part, parts.at[other], part_send.at[step], part_recv.at[step], layer_peer(-step)
        )

    for step in range(1, 8):
        part_copy(step).start()
    parts[layer] = own_part[...]
    for band in range(3):
        swap(band).wait_send()
    for d in range(4):
        cross(d).wait_send()
        code_copy(1, d).wait_send()

        @pl.when(jnp.logical_not(core * 4 + d == layer))
        def _(d=d):
            code_copy(0, d).wait_send()

    for step in range(1, 8):
        plane_copy(step).wait_send()
        line_copy(step).wait_send()
    for step in range(1, 8):
        part_arrival(step).wait_recv()
    total = parts[0]
    for k in range(1, 8):
        total = total + parts[k]
    commands_ref[...] = total
    for step in range(1, 8):
        part_copy(step).wait_send()


def publish_kernel(slopes_in, commands_in, slopes_ref, commands_ref, sem):
    copies = [
        pltpu.make_async_copy(slopes_in, slopes_ref, sem.at[0]),
        pltpu.make_async_copy(commands_in, commands_ref, sem.at[1]),
    ]
    for copy in copies:
        copy.start()
    for copy in copies:
        copy.wait()


def publish(slopes, commands):
    return pl.pallas_call(
        publish_kernel,
        out_shape=(
            jax.ShapeDtypeStruct(slopes.shape, F32),
            jax.ShapeDtypeStruct(commands.shape, F32),
        ),
        in_specs=[pl.BlockSpec(memory_space=pltpu.HBM)] * 2,
        out_specs=[pl.BlockSpec(memory_space=pltpu.HBM)] * 2,
        scratch_shapes=[pltpu.SemaphoreType.DMA((2,))],
        compiler_params=pltpu.CompilerParams(vmem_limit_bytes=66_900_000),
        name="publish",
    )(slopes, commands)


def on_device(screens, wind_shift, cone_offset, cone_weight, valid_mask, reconstructor):
    dma = pltpu.SemaphoreType.DMA
    matrix = reconstructor.reshape(3840, 2, 2, 128).transpose(0, 2, 1, 3).reshape(15360, 128)
    slopes, commands = pl.pallas_call(
        frame_kernel,
        out_shape=(
            jax.ShapeDtypeStruct((1, STARS, 2, 10), F32),
            jax.ShapeDtypeStruct((1, 256), F32),
        ),
        in_specs=[pl.BlockSpec(memory_space=pltpu.HBM)] * 6,
        out_specs=[pl.BlockSpec(memory_space=pltpu.VMEM)] * 2,
        scratch_shapes=[
            pltpu.SMEM((2, 32), jnp.int32),
            pltpu.SMEM((STARS, 32), jnp.int32),
            pltpu.SMEM((STARS, 32), F32),
            pltpu.VMEM((1, 10), jnp.int32),
            pltpu.VMEM((64, 2048), F32),
            pltpu.VMEM((64 * 11, 8, 128), F32),
            pltpu.VMEM((3, 8, 128, 128), jnp.int16),
            pltpu.VMEM((3, 4, 128, 128), jnp.int16),
            pltpu.VMEM((4, 128, 128), jnp.int16),
            pltpu.VMEM((3, 4, 128, 128), jnp.int16),
            pltpu.VMEM((2, 4, 128, 128), jnp.int16),
            pltpu.VMEM((2, 128, 128), BF16),
            pltpu.VMEM((128, 128), BF16),
            pltpu.VMEM((256, 384), BF16),
            pltpu.VMEM((1, 384), F32),
            pltpu.VMEM((8, 192), F32),
            pltpu.VMEM((2, 16, 192), F32),
            pltpu.VMEM((8, 1, 256), F32),
            pltpu.VMEM((8, 8, 1, 256), F32),
            pltpu.VMEM((15360, 128), BF16),
            pltpu.VMEM((1, 256), F32),
            pltpu.VMEM((8, 1, 256), F32),
            dma((6,)),
            dma((3,)),
            dma((3,)),
            dma((4,)),
            dma((4,)),
            dma((2, 4)),
            dma((2, 4)),
            dma((8,)),
            dma((8,)),
            dma((8,)),
            dma((8,)),
            dma((8,)),
            dma((8,)),
        ],
        compiler_params=pltpu.CompilerParams(
            collective_id=0, has_side_effects=True, vmem_limit_bytes=66_900_000
        ),
        name="frame",
    )(
        wind_shift.T,
        cone_offset,
        cone_weight,
        valid_mask,
        screens.reshape(64, 2048),
        matrix,
    )
    slopes, commands = publish(slopes, commands)
    return slopes, commands.reshape(-1)


def solution(mesh):
    placed = (
        P("layer", "tile", None),
        P(),
        P(),
        P(),
        P("tile", "layer"),
        P("layer", None, None, None, "tile"),
    )
    return jax.shard_map(
        on_device,
        mesh=mesh,
        in_specs=placed,
        out_specs=(P("tile", None, None, "layer"), P("tile")),
        check_vma=False,
    )
```

```python
import math

import jax
import jax.numpy as jnp
from jax import lax
from jax.experimental import pallas as pl
from jax.experimental.pallas import tpu as pltpu
from jax.sharding import PartitionSpec as P

STARS = 6
SPAN = 160
TILES = 64
UNIT = 2.0 * math.pi / 65536.0
MESH = pl.DeviceIdType.MESH
F32 = jnp.float32
BF16 = jnp.bfloat16
SINE = (
    1.5707962900208665,
    -0.6459633598429161,
    0.07968848044711395,
    -0.0046722277849454265,
    0.00015082049685476598,
)


def modulo_16(q):
    return ((q + 32768) & 65535) - 32768


def iota(shape, axis):
    return lax.broadcasted_iota(jnp.int32, shape, axis)


def split(x):
    high = x.astype(BF16)
    return high, (x - high.astype(F32)).astype(BF16)


def dot(a, b):
    return jnp.dot(a, b, preferred_element_type=F32)


def sine(q):
    q = jnp.where(q > 16384, 32768 - q, jnp.where(q < -16384, -32768 - q, q))
    x = q.astype(F32) * (1.0 / 16384.0)
    square = x * x
    value = SINE[4]
    for coefficient in SINE[3::-1]:
        value = value * square + coefficient
    return value * x


def filter_tables():
    row = iota((128, 128), 0)
    col = iota((128, 128), 1)
    gap = row - col
    same = (row >> 4) == (col >> 4)
    sign = jnp.where((gap & 1) == 0, 1.0, -1.0)
    angle = gap.astype(F32) * (math.pi / 32.0)
    inside = jnp.where(same & (gap != 0), angle, math.pi / 2.0)
    cotangent = jnp.cos(inside) / jnp.sin(inside)
    flips = jnp.where(same, sign, 0.0)
    odd = jnp.where(same & (gap != 0), -16.0 * sign * cotangent, 0.0)
    return flips, odd


def frame_kernel(
    wind_hbm,
    offset_hbm,
    weight_hbm,
    mask_hbm,
    screens_hbm,
    matrix_hbm,
    slopes_hbm,
    parts,
    slopes_ref,
    wind,
    cone_offset,
    cone_weight,
    mask_ref,
    held,
    placed,
    partial,
    swapped,
    crossed,
    coded,
    landed,
    filters,
    low_filter,
    pick_ref,
    lit_ref,
    expand,
    keep,
    gathered,
    matrix,
    own_part,
    load_sem,
    result_sem,
    swap_send,
    swap_recv,
    cross_send,
    cross_recv,
    code_send,
    code_recv,
    row_send,
    row_recv,
    part_send,
    part_recv,
):
    tile = lax.axis_index("tile")
    layer = lax.axis_index("layer")
    chip_y = layer // 2
    core = layer % 2
    half = layer // 4
    along = tile // 8

    def at(tile_index, layer_index):
        return (tile_index, layer_index)

    partner = at(tile, layer + 1 - 2 * core)
    side = tile % 2
    near_tile = tile + 1 - 2 * side
    near_band = 2 - 2 * side
    far_band = 2 * side
    onward = at((tile + 4 * side - 2 + TILES) % TILES, layer)
    backward = at((tile - 4 * side + 2 + TILES) % TILES, layer)

    def code_target(near, d):
        return at(near_tile if near else tile, core * 4 + d)

    def code_source(near, y):
        return at(near_tile if near else tile, y * 2 + half)

    def tile_peer(step):
        return at((tile + step) % TILES, layer)

    def layer_peer(step):
        return at(tile, (layer + step + 8) % 8)

    barrier = pltpu.get_barrier_semaphore()
    loads = [
        pltpu.make_async_copy(source, target, load_sem.at[k])
        for k, (source, target) in enumerate(
            (
                (wind_hbm, wind),
                (offset_hbm, cone_offset),
                (weight_hbm, cone_weight),
                (screens_hbm.at[0:16], held.at[0:16]),
                (screens_hbm.at[16:32], held.at[16:32]),
                (screens_hbm.at[32:48], held.at[32:48]),
                (screens_hbm.at[48:64], held.at[48:64]),
                (mask_hbm, mask_ref),
                (matrix_hbm, matrix),
            )
        )
    ]
    for load in loads[:8]:
        load.start()

    def greet(where):
        pl.semaphore_signal(barrier, inc=1, device_id=where, device_id_type=MESH)

    own_is_target = half == core
    for step in (4, 3, 5, 2, 6, 1, 7):
        greet(layer_peer(step))
    for y in range(4):
        greet(code_source(True, y))
    greet(backward)

    def greet_tile(step, carry):
        greet(tile_peer(step))
        return carry

    lax.fori_loop(1, TILES, greet_tile, 0)

    zeros = jnp.zeros((5, 8, 128), F32)

    def clear(k, carry):
        placed[pl.ds(11 * k, 5)] = zeros
        placed[pl.ds(11 * k + 8, 3)] = zeros[0:3]
        return carry

    lax.fori_loop(0, 64, clear, 0, unroll=8)
    for load in loads[:3]:
        load.wait()
    row = iota((8, 128), 0)
    for slot in range(4):
        loads[3 + slot].wait()
        down = (wind[0, layer * 4 + slot] + 16) & 7
        early = row < down
        for m in range(16):
            columns = slice(128 * m, 128 * m + 128)
            upper = pltpu.roll(held[16 * slot : 16 * slot + 8, columns], down, axis=0)
            lower = pltpu.roll(held[16 * slot + 8 : 16 * slot + 16, columns], down, axis=0)
            group = 11 * (16 * slot + m) + 5
            placed[group] = jnp.where(early, 0.0, upper)
            placed[group + 1] = jnp.where(early, upper, lower)
            placed[group + 2] = jnp.where(early, lower, 0.0)

    loads[8].start()
    lane = iota((16, 128), 1)

    def add_layers(band):
        tails = [None] * 8
        for star in range(STARS):
            total = [None] * 10
            for slot in range(4):
                which = layer * 4 + slot
                beginning = wind[1, which] + cone_offset[star, which]
                weight = cone_weight[star, which]
                column = lax.shift_right_logical(beginning, 7) + 16 * slot
                first = 11 * column + 5 - lax.shift_right_logical(wind[0, which] + 16, 3)
                first = first + 2 * band
                turn = beginning & 127
                roll_by = (128 - turn) & 127
                stay = lane < 128 - turn

                def turned(m, first=first, roll_by=roll_by):
                    window = placed[pl.ds(first + 11 * m, 2)].reshape(16, 128)
                    return pltpu.roll(window, roll_by, axis=1)

                before = turned(0)
                for m in range(10):
                    after = turned(m + 1)
                    term = weight * jnp.where(stay, before, after)
                    total[m] = term if slot == 0 else total[m] + term
                    before = after
            code = [jnp.round(part * (1.0 / UNIT)).astype(jnp.int32) for part in total]
            for block in range(8):
                tile_at, start = (block * SPAN) // 128, (block * SPAN) % 128
                main = code[tile_at]
                if start > 0:
                    main = jnp.where(
                        lane < 128 - start,
                        pltpu.roll(main, 128 - start, axis=1),
                        pltpu.roll(code[tile_at + 1], 128 - start, axis=1),
                    )
                place = 32 * (star % 4)
                tail = code[tile_at + 1]
                if place != start:
                    tail = pltpu.roll(tail, (place - start) % 128, axis=1)
                tail = jnp.where((lane >= place) & (lane < place + 32), tail, 0)
                tails[block] = tail if star % 4 == 0 else tails[block] + tail
                partial[band, block, 16 * star : 16 * star + 16, :] = main.astype(jnp.int16)
                if star in (3, 5):
                    at_row = 96 + 16 * (star // 4)
                    partial[band, block, at_row : at_row + 16, :] = tails[block].astype(jnp.int16)

    def remote(source, target, send, recv, where):
        return pltpu.make_async_remote_copy(
            src_ref=source,
            dst_ref=target,
            send_sem=send,
            recv_sem=recv,
            device_id=where,
            device_id_type=MESH,
        )

    def swap(band):
        return remote(
            partial.at[band, pl.ds((1 - core) * 4, 4)],
            swapped.at[band],
            swap_send.at[band],
            swap_recv.at[band],
            partner,
        )

    def cross(d):
        return remote(
            coded.at[far_band, d], crossed.at[d], cross_send.at[d], cross_recv.at[d], onward
        )

    def code_copy(near, d):
        return remote(
            coded.at[near_band if near else 1, d],
            landed.at[near, chip_y],
            code_send.at[near, d],
            code_recv.at[near, chip_y],
            code_target(near, d),
        )

    def code_arrival(near, y):
        return remote(
            coded.at[near_band if near else 1, 0],
            landed.at[near, y],
            code_send.at[near, 0],
            code_recv.at[near, y],
            code_source(near, y),
        )

    def both(band, d):
        own = partial[band, core * 4 + d].astype(jnp.int32)
        return own + swapped[band, d].astype(jnp.int32)

    add_layers(far_band)
    add_layers(1)
    pl.semaphore_wait(barrier, 12 + TILES - 1)
    swap(far_band).start()
    swap(1).start()
    add_layers(near_band)
    swap(near_band).start()
    swap(far_band).wait_recv()
    for d in range(4):
        coded[far_band, d] = both(far_band, d).astype(jnp.int16)
        cross(d).start()
    swap(1).wait_recv()
    for d in range(4):
        coded[1, d] = both(1, d).astype(jnp.int16)
    for d in range(4):
        is_self = core * 4 + d == layer

        @pl.when(jnp.logical_not(is_self))
        def _(d=d):
            code_copy(0, d).start()

        @pl.when(is_self)
        def _(d=d):
            landed[0, chip_y] = coded[1, d]

    swap(near_band).wait_recv()
    for d in range(4):
        cross(d).wait_recv()
        total = both(near_band, d) + crossed[d].astype(jnp.int32)
        coded[near_band, d] = total.astype(jnp.int16)
        code_copy(1, d).start()

    flips, odd = filter_tables()
    odd_high, odd_low = split(odd)
    filters[0] = flips.astype(BF16)
    filters[1] = odd_high
    low_filter[...] = odd_low
    column = iota((256, 384), 1)
    column = jnp.where(column < 128, column, (column - 128) >> 4)
    source = iota((256, 384), 0)
    wanted = jnp.where(source < 128, source >> 4, 8 + ((source >> 4) & 1))
    pick_ref[...] = jnp.where(wanted == column, 1.0 / 8192.0, 0.0).astype(BF16)
    spread = jnp.where(iota((10, 384), 0) == column[0:10], 1.0, 0.0)
    loads[7].wait()
    lit_ref[...] = dot(mask_ref[...].astype(F32), spread)
    place = iota((8, 192), 1)
    begin = 24 * iota((8, 192), 0)
    expand[...] = jnp.where((place >= begin) & (place < begin + 24), 1.0, 0.0)
    place = iota((16, 192), 1)
    entry = ((place >> 2) % 6) * 2 + (place & 1)
    for h in range(2):
        wanted = (entry == iota((16, 192), 0)) & (((place >> 1) & 1) == h)
        keep[h] = jnp.where(wanted, 1.0, 0.0)
    loads[8].wait()

    code = jnp.zeros((128, 128), jnp.int32)
    for y in range(4):
        @pl.when(jnp.logical_not(own_is_target & (chip_y == y)))
        def _(y=y):
            code_arrival(0, y).wait_recv()

    for y in range(4):
        code = code + landed[0, y].astype(jnp.int32)
    for y in range(4):
        code_arrival(1, y).wait_recv()
        code = code + landed[1, y].astype(jnp.int32)
    code = modulo_16(code)
    field_imag = sine(code)
    field_real = sine(modulo_16(code + 16384))
    real_high, real_low = split(field_real)
    imag_high, imag_low = split(field_imag)
    right = jnp.concatenate([filters[0], filters[1]], axis=1)
    across = dot(jnp.concatenate([real_high, real_low, imag_high, imag_low], axis=0), right)
    flipped_real = across[0:128, 0:128] + across[128:256, 0:128]
    flipped_imag = across[256:384, 0:128] + across[384:512, 0:128]
    turned_real = (
        across[0:128, 128:256] + across[128:256, 128:256] + dot(real_high, low_filter[...])
    )
    along_cols = (
        -16.0 * (field_real * flipped_real + field_imag * flipped_imag)
        - 2.0 * field_imag * turned_real
    )
    left = jnp.concatenate([filters[0], filters[1]], axis=0)
    down = dot(left, jnp.concatenate([real_high, real_low, imag_high, imag_low], axis=1))
    flipped_real = down[0:128, 0:128] + down[0:128, 128:256]
    flipped_imag = down[0:128, 256:384] + down[0:128, 384:512]
    turned_real = (
        down[128:256, 0:128] + down[128:256, 128:256] + dot(low_filter[...], real_high)
    )
    along_rows = (
        -16.0 * (field_real * flipped_real + field_imag * flipped_imag)
        + 2.0 * field_imag * turned_real
    )

    lane_8 = iota((8, 128), 1)
    row_8 = iota((8, 128), 0)
    sums = []
    for moment in (along_cols, along_rows):
        blocks = jnp.sum(moment.reshape(8, 16, 128), axis=1)
        shared = jnp.where(row_8 < 4, blocks[6:7, :], blocks[7:8, :])
        shared = jnp.where((lane_8 >> 5) == (row_8 & 3), shared, 0.0)
        sums.append(jnp.concatenate([blocks, shared], axis=1))
    sums = jnp.concatenate(sums, axis=0)
    high, rest = sums.astype(BF16), sums
    rest = rest - high.astype(F32)
    middle, low = split(rest)
    measured = dot(jnp.concatenate([high, middle, low], axis=0), pick_ref[...])
    measured = (measured[0:16] + measured[16:32] + measured[32:48]) * lit_ref[...]
    for star in range(STARS):
        for axis in range(2):
            slopes_ref[0, star, axis, :] = measured[axis * 8 + star, 0:10]
    slopes_out = pltpu.make_async_copy(slopes_ref, slopes_hbm, result_sem.at[0])
    slopes_out.start()
    lane_16 = iota((16, 256), 1)
    row_16 = iota((16, 256), 0)
    entry = (row_16 & 7) * 2 + (row_16 >> 3)
    coarse = measured[:, 128:384].astype(BF16).astype(F32)
    flat = jnp.where(((lane_16 & 15) == entry) & (entry < 12), coarse, 0.0)
    gathered[tile] = jnp.sum(flat, axis=0, keepdims=True)

    def row_copy(step):
        return remote(
            gathered.at[tile],
            gathered.at[tile],
            row_send,
            row_recv.at[along],
            tile_peer(step),
        )

    def send_row(step, carry):
        row_copy(step).start()
        return carry

    lax.fori_loop(8, TILES, send_row, 0)
    lax.fori_loop(1, 8, send_row, 0)

    def rows_wait(first, count, z):
        rows = gathered.at[pl.ds(first, count)]
        return remote(rows, rows, row_send, row_recv.at[z], tile_peer(1))

    total = jnp.zeros((32, 128), F32)
    for other in range(8):
        @pl.when(along != other)
        def _(other=other):
            rows_wait(8 * other, 8, other).wait_recv()

        @pl.when(along == other)
        def _(other=other):
            rows_wait(8 * other, 7, other).wait_recv()

        rows = lax.dot_general(
            gathered[8 * other : 8 * other + 8].reshape(8, 256)[:, 0:160],
            expand[...],
            (((0,), (0,)), ((), ())),
            preferred_element_type=F32,
        )
        for j in range(10):
            block = rows[16 * j : 16 * j + 16]
            vector = jnp.concatenate([block * keep[0], block * keep[1]], axis=0).astype(BF16)
            start = 1536 * j + 192 * other
            total = total + dot(vector, matrix[start : start + 192, :])
    own_part[...] = jnp.concatenate(
        [
            jnp.sum(total[0:16], axis=0, keepdims=True),
            jnp.sum(total[16:32], axis=0, keepdims=True),
        ],
        axis=1,
    )

    def part_copy(step):
        return remote(
            own_part, parts.at[layer], part_send.at[step], part_recv.at[step], layer_peer(step)
        )

    def part_arrival(step):
        other = (layer - step + 8) % 8
        return remote(
            own_part, parts.at[other], part_send.at[step], part_recv.at[step], layer_peer(-step)
        )

    for step in range(1, 8):
        part_copy(step).start()
    part_out = pltpu.make_async_copy(own_part, parts.at[layer], result_sem.at[1])
    part_out.start()
    for band in range(3):
        swap(band).wait_send()
    for d in range(4):
        cross(d).wait_send()
        code_copy(1, d).wait_send()

        @pl.when(jnp.logical_not(core * 4 + d == layer))
        def _(d=d):
            code_copy(0, d).wait_send()

    rows_wait(0, TILES - 1, 0).wait_send()
    slopes_out.wait()
    part_out.wait()
    for step in range(1, 8):
        part_arrival(step).wait_recv()
    for step in range(1, 8):
        part_copy(step).wait_send()


def publish_kernel(slopes_in, parts_in, slopes_ref, commands_ref, parts, total, sem):
    slopes_copy = pltpu.make_async_copy(slopes_in, slopes_ref, sem.at[0])
    slopes_copy.start()
    load = pltpu.make_async_copy(parts_in, parts, sem.at[1])
    load.start()
    load.wait()
    added = parts[0]
    for k in range(1, 8):
        added = added + parts[k]
    total[...] = added
    store = pltpu.make_async_copy(total, commands_ref, sem.at[2])
    store.start()
    store.wait()
    slopes_copy.wait()


def publish(slopes, parts):
    return pl.pallas_call(
        publish_kernel,
        out_shape=(
            jax.ShapeDtypeStruct(slopes.shape, F32),
            jax.ShapeDtypeStruct((1, 256), F32),
        ),
        in_specs=[pl.BlockSpec(memory_space=pltpu.HBM)] * 2,
        out_specs=[pl.BlockSpec(memory_space=pltpu.HBM)] * 2,
        scratch_shapes=[
            pltpu.VMEM((8, 1, 256), F32),
            pltpu.VMEM((1, 256), F32),
            pltpu.SemaphoreType.DMA((3,)),
        ],
        compiler_params=pltpu.CompilerParams(vmem_limit_bytes=66_900_000),
        name="publish",
    )(slopes, parts)


def on_device(screens, wind_shift, cone_offset, cone_weight, valid_mask, reconstructor):
    dma = pltpu.SemaphoreType.DMA
    matrix = reconstructor.reshape(3840, 2, 2, 128).transpose(0, 2, 1, 3).reshape(15360, 128)
    slopes, parts = pl.pallas_call(
        frame_kernel,
        out_shape=(
            jax.ShapeDtypeStruct((1, STARS, 2, 10), F32),
            jax.ShapeDtypeStruct((8, 1, 256), F32),
        ),
        in_specs=[pl.BlockSpec(memory_space=pltpu.HBM)] * 6,
        out_specs=[pl.BlockSpec(memory_space=pltpu.HBM)] * 2,
        scratch_shapes=[
            pltpu.VMEM((1, STARS, 2, 10), F32),
            pltpu.SMEM((2, 32), jnp.int32),
            pltpu.SMEM((STARS, 32), jnp.int32),
            pltpu.SMEM((STARS, 32), F32),
            pltpu.VMEM((1, 10), jnp.int32),
            pltpu.VMEM((64, 2048), F32),
            pltpu.VMEM((64 * 11, 8, 128), F32),
            pltpu.VMEM((3, 8, 128, 128), jnp.int16),
            pltpu.VMEM((3, 4, 128, 128), jnp.int16),
            pltpu.VMEM((4, 128, 128), jnp.int16),
            pltpu.VMEM((3, 4, 128, 128), jnp.int16),
            pltpu.VMEM((2, 4, 128, 128), jnp.int16),
            pltpu.VMEM((2, 128, 128), BF16),
            pltpu.VMEM((128, 128), BF16),
            pltpu.VMEM((256, 384), BF16),
            pltpu.VMEM((1, 384), F32),
            pltpu.VMEM((8, 192), F32),
            pltpu.VMEM((2, 16, 192), F32),
            pltpu.VMEM((TILES, 1, 256), F32),
            pltpu.VMEM((15360, 128), BF16),
            pltpu.VMEM((1, 256), F32),
            dma((9,)),
            dma((2,)),
            dma((3,)),
            dma((3,)),
            dma((4,)),
            dma((4,)),
            dma((2, 4)),
            dma((2, 4)),
            dma,
            dma((8,)),
            dma((8,)),
            dma((8,)),
        ],
        compiler_params=pltpu.CompilerParams(
            collective_id=0, has_side_effects=True, vmem_limit_bytes=66_900_000
        ),
        name="frame",
    )(
        wind_shift.T,
        cone_offset,
        cone_weight,
        valid_mask,
        screens.reshape(64, 2048),
        matrix,
    )
    slopes, commands = publish(slopes, parts)
    return slopes, commands.reshape(-1)


def solution(mesh):
    placed = (
        P("layer", "tile", None),
        P(),
        P(),
        P(),
        P("tile", "layer"),
        P("layer", None, None, None, "tile"),
    )
    return jax.shard_map(
        on_device,
        mesh=mesh,
        in_specs=placed,
        out_specs=(P("tile", None, None, "layer"), P("tile")),
        check_vma=False,
    )
```
